32 devices in a mesh: row: 4 (over x, core), col: 8 (over z, y).
Axes of the slice: x: 2, y: 2, z: 4, core: 2. Of those that a mesh axis runs over, the one named last changes fastest.
Arguments:
- front_matrix: float32 [32, 4, 128, 16, 8, 128], P(None, 'row', None, None, 'col'), as said below
- children: bfloat16 [2, 4, 4, 128, 16, 8, 128], P(None, None, 'row', None, None, 'col'), may hold values from -0.5 to 0.5
- child_map: int32 [2, 16], replicated, may hold values from 0 to 127, as said below
- row_order: int32 [2, 16, 128], replicated, may hold values from 0 to 127, each once within a row
Outputs:
- schur_part: float32 [32, 4, 128, 16, 8, 128], P(None, 'row', None, None, 'col')
- factor_part: float32 [32, 4, 128, 1536], P('col', 'row')
The draws below stay inside these ranges and needn't reach their ends.
Inputs may be any that keep to these rules, and one draw needn't show every extreme that they name: `front_matrix`: Off-diagonal entries lie within -1.2 and 1.2 + 0.3 * sqrt(16384); diagonal entries lie between 2.5 and 3.9 times the square root of 16384. The lower triangle, with the children's rows added and mirrored, is positive definite. `child_map`: each child sends its tile rows to distinct front tile rows. Of the 4 tile rows of one child held by one device row, at most 2 go to any one device row (front tile row modulo 4), and exactly 2 go to some device row.
All inputs are finite; a program needn't handle non-finite values.
Results may differ from the reference program's by a relative error of at most 0.001.
Values may be sent and summed in bfloat16 or wider, within the bound.
No kernel may reach another device: no remote copies, remote signals or barrier semaphores. Data moves between devices by JAX's collectives and lax.ppermute only.
A program may use at most 384 MiB of HBM per device.

```python
import jax
import jax.numpy as jnp
from jax import lax

F = 16384
TILE = 128
PWT = 4
STEPS = 3
CAP = 2
PW = 512
LR = 32
LC = 16
LRC = 4
NTC = 16
N_ROW = 4
N_COL = 8


def draw_front_matrix(key, part):
    shape = (LR, N_ROW, TILE, LC, N_COL, TILE)
    key_off = jax.random.fold_in(key, 1)
    key_diag = jax.random.fold_in(key, 2)
    key_site = jax.random.fold_in(key, 3)
    row_index = (lax.broadcasted_iota(jnp.int32, (LR, N_ROW, TILE, 1, 1, 1), 0) * N_ROW + lax.broadcasted_iota(jnp.int32, (LR, N_ROW, TILE, 1, 1, 1), 1)) * TILE + lax.broadcasted_iota(jnp.int32, (LR, N_ROW, TILE, 1, 1, 1), 2)
    col_index = (lax.broadcasted_iota(jnp.int32, (1, 1, 1, LC, N_COL, TILE), 3) * N_COL + lax.broadcasted_iota(jnp.int32, (1, 1, 1, LC, N_COL, TILE), 4)) * TILE + lax.broadcasted_iota(jnp.int32, (1, 1, 1, LC, N_COL, TILE), 5)
    scale_root = jnp.sqrt(jnp.float32(F))
    sites = jax.random.uniform(key_site, (3, F), jnp.float32, 0.0, 1.0)
    first_gap = sites[0][row_index] - sites[0][col_index]
    second_gap = sites[1][row_index] - sites[1][col_index]
    third_gap = sites[2][row_index] - sites[2][col_index]
    squared = first_gap * first_gap + second_gap * second_gap + third_gap * third_gap
    ratio = jnp.sqrt(squared) / 0.6
    falloff = jnp.maximum(1.0 - ratio, 0.0)
    falloff_sq = falloff * falloff
    kernel = falloff_sq * falloff_sq * (4.0 * ratio + 1.0)
    off_diag = jax.random.uniform(key_off, shape, jnp.float32, -1.0, 1.0)
    diag_vals = jax.random.uniform(key_diag, shape, jnp.float32, 2.4, 3.6) * scale_root
    base = jnp.where(row_index == col_index, diag_vals, off_diag)
    return base + 0.3 * scale_root * kernel


def child_slots(subkey):
    key_src = jax.random.fold_in(subkey, 11)
    key_dst = jax.random.fold_in(subkey, 12)

    def per_source(source_key):
        key_perm = jax.random.fold_in(source_key, 1)
        key_first = jax.random.fold_in(source_key, 2)
        scores = jax.random.permutation(key_perm, N_ROW * CAP)
        forced = jax.random.randint(key_first, (), 0, N_ROW)
        slot_ids = jnp.arange(N_ROW * CAP, dtype=jnp.int32)
        scores = jnp.where(slot_ids // CAP == forced, -1 - slot_ids, scores)
        return jnp.argsort(scores, stable=True)[:LRC].astype(jnp.int32)
    chosen = jax.vmap(per_source)(jax.random.split(key_src, N_ROW))
    dest_rows = chosen // CAP
    position = jnp.arange(N_ROW, dtype=jnp.int32)[:, None] * CAP + chosen % CAP
    local_perms = jax.vmap(lambda one_key: jax.random.permutation(one_key, LR))(jax.random.split(key_dst, N_ROW)).astype(jnp.int32)
    local_rows = local_perms[dest_rows, position]
    mapped = local_rows * N_ROW + dest_rows
    return mapped.T.reshape(-1).astype(jnp.int32)


def draw_child_map(key, part):
    return jnp.stack([child_slots(jax.random.fold_in(key, 101)), child_slots(jax.random.fold_in(key, 202))])


def block_levels(own_key, dims, cuts, least, high):
    level = 1.0
    for dim, shards_of in cuts:
        heights = jax.random.uniform(jax.random.fold_in(jax.random.fold_in(own_key, 6), dim), (shards_of,), jnp.float32, least / len(cuts), high / len(cuts))
        level = level * jnp.repeat(jnp.exp(heights), dims[dim] // shards_of).reshape((-1,) + (1,) * (len(dims) - 1 - dim))
    return level


def setup_inputs(seed: int = 0) -> dict:
    seeds = jax.random.split(jax.random.key(seed), 5)
    return {
        "front_matrix": draw_front_matrix(jax.random.fold_in(seeds[4], 71), 0),
        "children": jnp.clip(jax.random.uniform(seeds[1], (2, LRC, N_ROW, TILE, LC, N_COL, TILE), jnp.float32, -0.5, 0.5) * block_levels(seeds[1], (2, LRC, N_ROW, TILE, LC, N_COL, TILE), ((2, 4), (5, 8)), -0.4, 0.0), -0.5, 0.5).astype(jnp.bfloat16),
        "child_map": draw_child_map(jax.random.fold_in(seeds[4], 71), 0),
        "row_order": jax.vmap(lambda own: jax.random.permutation(own, TILE))(jax.random.split(seeds[3], 2 * NTC)).reshape((2, NTC, TILE)).astype(jnp.int32),
    }


def mirror_lower(block):
    return jnp.tril(block) + jnp.tril(block, -1).T

def reference(front_matrix, children, child_map, row_order):
    full_order = LR * N_ROW * TILE
    matrix = front_matrix.reshape(full_order, full_order)
    child_rows = children.reshape(2, NTC * TILE, full_order).astype(jnp.float32)
    for child_index in range(2):
        targets = (child_map[child_index][:, None] * TILE + row_order[child_index]).reshape(-1).astype(jnp.int32)
        matrix = matrix.at[targets].add(child_rows[child_index])
    positions = jnp.arange(full_order, dtype=jnp.int32)
    factors = []
    for panel_index in range(STEPS):
        first_col = panel_index * PW
        diagonal = mirror_lower(matrix[first_col:first_col + PW, first_col:first_col + PW])
        cholesky_factor = jnp.linalg.cholesky(diagonal)
        columns = matrix[:, first_col:first_col + PW]
        solved = jax.scipy.linalg.solve_triangular(cholesky_factor, columns.T, lower=True).T
        solved = jnp.where(positions[:, None] < first_col, jnp.zeros_like(solved), solved)
        solved = solved.at[first_col:first_col + PW].set(cholesky_factor)
        matrix = matrix - jnp.dot(solved, solved.T, precision=lax.Precision.HIGHEST)
        factors.append(solved)
    tile_index = positions // TILE
    kept_mask = (tile_index[:, None] >= tile_index[None, :]) & (tile_index[None, :] >= STEPS * PWT)
    schur_part = jnp.where(kept_mask, matrix, jnp.zeros_like(matrix)).reshape(front_matrix.shape)
    factor_part = jnp.concatenate(factors, axis=1).reshape(LR, N_ROW, TILE, STEPS * PW)
    return (schur_part, factor_part)
```

```python
import functools

import jax
import jax.numpy as jnp
from jax import lax
from jax.experimental import pallas as pl
from jax.experimental.pallas import tpu as pltpu
from jax.sharding import PartitionSpec as P

PWT = 4
STEPS = 3
CAP = 2
TILES = PWT * STEPS
F32 = jnp.float32
BF16 = jnp.bfloat16
LINK = jnp.float16
VMEM_LIMIT = 60 * 1024 * 1024


def slot_ranks(mapping, row_count):
    indices = jnp.arange(mapping.shape[0], dtype=jnp.int32)
    sources = indices % row_count
    targets = mapping % row_count
    earlier = (
        (sources[:, None] == sources[None, :])
        & (targets[:, None] == targets[None, :])
        & (indices[None, :] < indices[:, None])
    )
    return (sources, targets, jnp.sum(earlier.astype(jnp.int32), axis=1))


def dot(a, b, contract):
    return lax.dot_general(a, b, (contract, ((), ())), preferred_element_type=F32)


NT = ((1,), (1,))
NN = ((1,), (0,))
TN = ((0,), (0,))


def halves(x):
    high = x.astype(BF16)
    return high, (x - high.astype(F32)).astype(BF16)


def dot3(a, b, contract):
    ah, al = halves(a)
    bh, bl = halves(b)
    return dot(ah, bh, contract) + (dot(al, bh, contract) + dot(ah, bl, contract))


def spread_lane(x, j):
    return jnp.broadcast_to(x[:, j : j + 1], (8, x.shape[1]))


def spread_row(x, i):
    return jnp.broadcast_to(x[i : i + 1, :], (8, x.shape[1]))


def factor_tile(tile):
    size = tile.shape[0]
    sub = lax.broadcasted_iota(jnp.int32, (8, size), 0)
    lane = lax.broadcasted_iota(jnp.int32, (8, size), 1)
    groups = size // 8
    left = [tile[8 * s : 8 * s + 8] for s in range(groups)]
    right = [jnp.where(lane == sub + 8 * s, 1.0, 0.0).astype(F32) for s in range(groups)]
    for s in range(groups):
        columns = [spread_lane(left[s], 8 * s + b) for b in range(8)]
        square = {(a, b): spread_row(columns[b], a) for a in range(8) for b in range(a + 1)}
        lrow = [spread_row(left[s], i) for i in range(8)]
        rrow = [spread_row(right[s], i) for i in range(8)]
        new_left = jnp.zeros((8, size), F32)
        new_right = jnp.zeros((8, size), F32)
        for i in range(8):
            inverse = lax.rsqrt(square[i, i])
            below = {a: square[a, i] * inverse for a in range(i + 1, 8)}
            lrow[i] = lrow[i] * inverse
            rrow[i] = rrow[i] * inverse
            for a in range(i + 1, 8):
                for b in range(i + 1, a + 1):
                    square[a, b] = square[a, b] - below[a] * below[b]
                lrow[a] = lrow[a] - below[a] * lrow[i]
                rrow[a] = rrow[a] - below[a] * rrow[i]
            new_left = jnp.where(sub == i, lrow[i], new_left)
            new_right = jnp.where(sub == i, rrow[i], new_right)
        left[s], right[s] = new_left, new_right
        if s < groups - 1:
            turned = new_left.T
            for t in range(s + 1, groups):
                for a in range(8):
                    scale = jnp.broadcast_to(turned[8 * t : 8 * t + 8, a : a + 1], (8, size))
                    left[t] = left[t] - scale * lrow[a]
                    right[t] = right[t] - scale * rrow[a]
    return jnp.concatenate(left, 0), jnp.concatenate(right, 0)


def whole(shape):
    return pl.BlockSpec(shape, lambda *_: (0,) * len(shape), pipeline_mode=pl.Buffered(1))


def pack_kernel(row_count, ids_ref, map_ref, kids_ref, out_ref):
    out_ref[...] = jnp.zeros(out_ref.shape, out_ref.dtype)
    for h in range(2):
        targets = []
        for i in range(kids_ref.shape[1]):
            target = map_ref[h, i * row_count + ids_ref[0]] % row_count
            rank = jnp.int32(0)
            for earlier in targets:
                rank = rank + (earlier == target).astype(jnp.int32)
            targets.append(target)
            out_ref[target, h, rank] = kids_ref[h, i]


def pack_children(ids, child_map, kids, row_count):
    return pl.pallas_call(
        functools.partial(pack_kernel, row_count),
        out_shape=jax.ShapeDtypeStruct((row_count, 2, CAP) + kids.shape[2:], kids.dtype),
        grid_spec=pltpu.PrefetchScalarGridSpec(
            num_scalar_prefetch=2,
            grid=(1,),
            in_specs=[whole(kids.shape)],
            out_specs=whole((row_count, 2, CAP) + kids.shape[2:]),
        ),
        compiler_params=pltpu.CompilerParams(vmem_limit_bytes=VMEM_LIMIT),
    )(ids, child_map, kids)


def panel_kernel(lpc, share, slot_ref, *refs):
    fronts = refs[:lpc]
    order_ref, recv_ref, high_ref, low_ref = refs[lpc:]
    tile = high_ref.shape[-1]
    rows = lax.broadcasted_iota(jnp.int32, (tile, tile), 0)
    for k in range(share):
        a = pl.program_id(0) * share + k
        moved = jnp.zeros((tile, lpc * tile), F32)
        for h in range(2):
            pick = (rows == order_ref[k, h : h + 1, :]).astype(BF16)
            moved = moved + dot(pick, recv_ref[slot_ref[h, a]], NN)
        for b in range(lpc):
            high, low = halves(fronts[b][k] + moved[:, b * tile : (b + 1) * tile])
            high_ref[k, b] = high
            low_ref[k, b] = low


def assemble_panel(fronts, order, slots, received):
    local_rows, tile, _ = fronts[0].shape
    lpc = len(fronts)
    share = 4 if local_rows % 4 == 0 else 1
    out = (local_rows, lpc, tile, tile)
    return pl.pallas_call(
        functools.partial(panel_kernel, lpc, share),
        out_shape=(jax.ShapeDtypeStruct(out, BF16), jax.ShapeDtypeStruct(out, BF16)),
        grid_spec=pltpu.PrefetchScalarGridSpec(
            num_scalar_prefetch=1,
            grid=(local_rows // share,),
            in_specs=[pl.BlockSpec((share, tile, tile), lambda a, s: (a, 0, 0))] * lpc
            + [
                pl.BlockSpec((share, 2, tile), lambda a, s: (a, 0, 0)),
                whole(received.shape),
            ],
            out_specs=[pl.BlockSpec((share,) + out[1:], lambda a, s: (a, 0, 0, 0))] * 2,
        ),
        compiler_params=pltpu.CompilerParams(vmem_limit_bytes=VMEM_LIMIT),
    )(slots, *fronts, order, received)


def lead_slots(row_count, col_count, lead_rows, lead_cols):
    return [
        (a, b)
        for a in range(lead_rows)
        for b in range(lead_cols)
        if col_count * b <= row_count * a + row_count - 1 and col_count * b < TILES
    ]


def unpack_kernel(row_count, col_count, slots, g_ref, *blocks):
    tile = g_ref.shape[-1]
    place = {ab: n for n, ab in enumerate(slots)}
    for i in range(TILES):
        for j in range(i + 1):
            n = place[i // row_count, j // col_count]
            t, u = i // PWT, j // PWT
            rows = pl.ds((i % PWT) * tile, tile)
            cols = pl.ds((j % PWT) * tile, tile)
            source = ((i % row_count) * col_count + j % col_count) * len(slots) + n
            blocks[t * (t + 1) // 2 + u][rows, cols] = g_ref[source]


def unpack_lead(gathered, row_count, col_count, slots):
    width = PWT * gathered.shape[-1]
    count = STEPS * (STEPS + 1) // 2
    return pl.pallas_call(
        functools.partial(unpack_kernel, row_count, col_count, slots),
        out_shape=[jax.ShapeDtypeStruct((width, width), F32)] * count,
        compiler_params=pltpu.CompilerParams(vmem_limit_bytes=VMEM_LIMIT),
    )(gathered)


def block_kernel(d_ref, l_ref, v_ref, vb_ref, work):
    width = d_ref.shape[0]
    tile = width // PWT
    row = lax.broadcasted_iota(jnp.int32, (tile, tile), 0)
    col = lax.broadcasted_iota(jnp.int32, (tile, tile), 1)
    work[...] = d_ref[...]
    l_ref[...] = jnp.zeros((width, width), F32)
    v_ref[...] = jnp.zeros((width, width), F32)
    for k in range(PWT):
        low, high = k * tile, (k + 1) * tile
        block = work[low:high, low:high]
        block = jnp.where(row >= col, block, block.T)
        upper, inverse = factor_tile(block)
        l_ref[low:high, low:high] = jnp.where(row <= col, upper, 0.0).T
        if k > 0:
            v_ref[low:high, 0:low] = dot3(inverse, v_ref[low:high, 0:low], NN)
        v_ref[low:high, low:high] = inverse
        if k < PWT - 1:
            below = dot3(work[high:width, low:high], inverse, NT)
            l_ref[high:width, low:high] = below
            work[high:width, high:width] -= dot3(below, below, NT)
            v_ref[high:width, 0:high] -= dot3(below, v_ref[low:high, 0:high], NN)
    vb_ref[...] = v_ref[...].astype(BF16)


def factor_block(diagonal):
    shape = diagonal.shape
    return pl.pallas_call(
        block_kernel,
        out_shape=(
            jax.ShapeDtypeStruct(shape, F32),
            jax.ShapeDtypeStruct(shape, F32),
            jax.ShapeDtypeStruct(shape, BF16),
        ),
        scratch_shapes=[pltpu.VMEM(shape, F32)],
        compiler_params=pltpu.CompilerParams(vmem_limit_bytes=VMEM_LIMIT),
        cost_estimate=pl.CostEstimate(flops=3 * 10**10, bytes_accessed=4 * 10**6, transcendentals=0),
    )(diagonal)


def advance_kernel(count, v_ref, *refs):
    below, trail = refs[:count], refs[count : count + count * (count + 1) // 2]
    rest = refs[count + len(trail) :]
    lower, lower_b, out = rest[:count], rest[count : 2 * count], rest[2 * count :]
    for t in range(count):
        lower[t][...] = dot3(below[t][...], v_ref[...], NT)
        lower_b[t][...] = lower[t][...].astype(BF16)
    for t in range(count):
        for u in range(t + 1):
            n = t * (t + 1) // 2 + u
            out[n][...] = trail[n][...] - dot3(lower[t][...], lower[u][...], NT)


def advance(inverse, below, trail):
    count = len(below)
    shape = inverse.shape
    kinds = [F32] * count + [BF16] * count + [F32] * len(trail)
    out = pl.pallas_call(
        functools.partial(advance_kernel, count),
        out_shape=[jax.ShapeDtypeStruct(shape, k) for k in kinds],
        compiler_params=pltpu.CompilerParams(vmem_limit_bytes=VMEM_LIMIT),
        cost_estimate=pl.CostEstimate(flops=3 * 10**9, bytes_accessed=10**7, transcendentals=0),
    )(inverse, *below, *trail)
    return out[:count], out[count : 2 * count], out[2 * count :]


def side_by_side(parts):
    return jnp.concatenate([p.reshape(-1, p.shape[-1]) for p in parts], axis=1)


def own_kernel(row_count, ids_ref, own_ref, l_ref, v_ref, out_ref):
    k = pl.program_id(0)
    tile = own_ref.shape[-1]
    width = PWT * tile
    index = (ids_ref[1] * pl.num_programs(0) + k) * row_count + ids_ref[0]

    @pl.when(index < TILES)
    def _():
        first = pl.multiple_of((index % PWT) * tile, tile)
        for s in range(STEPS):
            out_ref[0, :, s * width : (s + 1) * width] = l_ref[index // PWT, s, pl.ds(first, tile), :]

    @pl.when(index >= TILES)
    def _():
        solved = []
        for s in range(STEPS):
            rest = side_by_side([own_ref[s * PWT + j, 0] for j in range(PWT)])
            for q in range(s):
                rest = rest - dot3(solved[q], l_ref[s, q], NT)
            solved.append(dot3(rest, v_ref[s], NT))
            out_ref[0, :, s * width : (s + 1) * width] = solved[s]


def own_rows(ids, own, lower, inverse, row_count):
    tile = own.shape[-1]
    share = own.shape[1]
    return pl.pallas_call(
        functools.partial(own_kernel, row_count),
        out_shape=jax.ShapeDtypeStruct((share, tile, TILES * tile), F32),
        grid_spec=pltpu.PrefetchScalarGridSpec(
            num_scalar_prefetch=1,
            grid=(share,),
            in_specs=[
                pl.BlockSpec((TILES, 1, tile, tile), lambda k, s: (0, k, 0, 0)),
                whole(lower.shape),
                whole(inverse.shape),
            ],
            out_specs=pl.BlockSpec((1, tile, TILES * tile), lambda k, s: (k, 0, 0)),
        ),
        compiler_params=pltpu.CompilerParams(vmem_limit_bytes=VMEM_LIMIT),
    )(ids, own, lower, inverse)


def solve_kernel(first, n_parts, *refs):
    parts = refs[:n_parts]
    l_ref, v_ref, out_ref = refs[n_parts:]
    tile = parts[0].shape[-1]
    width = PWT * tile
    count = parts[0].shape[1]
    step = min(4, count)
    where = [(n, j) for n, ref in enumerate(parts) for j in range(ref.shape[0])]
    if first:
        out_ref[0 : first * tile, :] = jnp.zeros((first * tile, out_ref.shape[1]), BF16)

    @pl.loop(0, -(-count // step))
    def _(i):
        a = jnp.minimum(i * step, count - step)
        rows = pl.ds(pl.multiple_of((a + first) * tile, tile), step * tile)
        done = []
        for s in range(STEPS):
            pieces = [parts[n][j, pl.ds(a, step)] for n, j in where[s * PWT : (s + 1) * PWT]]
            rest = side_by_side(pieces)
            if s > 0:
                rest = rest.astype(F32)
                for q in range(s):
                    rest = rest - dot(done[q], l_ref[s * (s - 1) // 2 + q], NT)
                rest = rest.astype(BF16)
            done.append(dot(rest, v_ref[s], NT).astype(BF16))
            out_ref[rows, s * width : (s + 1) * width] = done[s]


def solve_rows(parts, first, lower, inverse):
    tile = parts[0].shape[-1]
    count = parts[0].shape[1]
    rows = (first + count) * tile
    return pl.pallas_call(
        functools.partial(solve_kernel, first, len(parts)),
        out_shape=jax.ShapeDtypeStruct((rows, TILES * tile), BF16),
        compiler_params=pltpu.CompilerParams(vmem_limit_bytes=VMEM_LIMIT),
        cost_estimate=pl.CostEstimate(
            flops=count * tile * (TILES * tile) ** 2 * 2,
            bytes_accessed=4 * rows * TILES * tile,
            transcendentals=0,
        ),
    )(*parts, lower, inverse)


def join_kernel(slot_ref, order_ref, recv_ref, front_ref, out_ref):
    g = pl.program_id(0)
    tile, local_cols = recv_ref.shape[1:3]
    share = out_ref.shape[0] // (tile * local_cols)
    out_ref[...] = front_ref[...]
    for k in range(share):
        a = g * share + k
        for h in range(2):
            slot = slot_ref[h, a]

            @pl.when(slot >= 0)
            def _(a=a, k=k, h=h, slot=slot):
                @pl.loop(0, tile, unroll=8)
                def _(t):
                    first = (k * tile + order_ref[h, a, t]) * local_cols
                    first = pl.multiple_of(first, local_cols)
                    out_ref[pl.ds(first, local_cols), :] += recv_ref[slot, t].astype(F32)


def join_children(slots, order, received, front, steps):
    rows = front.shape[0] // steps
    block = pl.BlockSpec((rows, front.shape[1]), lambda g, *_: (g, 0))
    return pl.pallas_call(
        join_kernel,
        out_shape=jax.ShapeDtypeStruct(front.shape, F32),
        grid_spec=pltpu.PrefetchScalarGridSpec(
            num_scalar_prefetch=2,
            grid=(steps,),
            in_specs=[whole(received.shape), block],
            out_specs=block,
        ),
        compiler_params=pltpu.CompilerParams(vmem_limit_bytes=VMEM_LIMIT),
        cost_estimate=pl.CostEstimate(flops=0, bytes_accessed=8 * front.size, transcendentals=0),
    )(slots, order, received, front)


def final_kernel(row_count, col_count, ids_ref, xr_ref, xc_ref, front_ref, out_ref):
    g = pl.program_id(0)
    tile = out_ref.shape[-1]
    share = xr_ref.shape[0] // tile
    local_cols = xc_ref.shape[0] // tile
    last = row_count * (g * share + share - 1) + ids_ref[0]
    pair = 2 if local_cols % 2 == 0 else 1
    for b in range(0, local_cols, pair):
        some = last >= jnp.maximum(col_count * b + ids_ref[1], TILES)

        @pl.when(some)
        def _(b=b):
            update = dot(xr_ref[...], xc_ref[b * tile : (b + pair) * tile, :], NT)
            for k in range(share):
                row_tile = row_count * (g * share + k) + ids_ref[0]
                for j in range(pair):
                    col_tile = col_count * (b + j) + ids_ref[1]
                    keep = (row_tile >= col_tile) & (col_tile >= TILES)
                    at = pl.ds(k * tile * local_cols + b + j, tile, stride=local_cols)
                    part = update[k * tile : (k + 1) * tile, j * tile : (j + 1) * tile]
                    out_ref[at, :] = jnp.where(keep, front_ref[at, :] - part, 0.0)

        @pl.when(jnp.logical_not(some))
        def _(b=b):
            for j in range(pair):
                out_ref[pl.ds(b + j, share * tile, stride=local_cols), :] = jnp.zeros(
                    (share * tile, tile), F32
                )


def final_update(ids, xr, xc, front, row_count, col_count):
    rows = front.shape[0] // col_count
    block = pl.BlockSpec((rows, front.shape[1]), lambda g, *_: (g, 0))
    return pl.pallas_call(
        functools.partial(final_kernel, row_count, col_count),
        out_shape=jax.ShapeDtypeStruct(front.shape, F32),
        grid_spec=pltpu.PrefetchScalarGridSpec(
            num_scalar_prefetch=1,
            grid=(col_count,),
            in_specs=[
                pl.BlockSpec((xr.shape[0] // col_count, xr.shape[1]), lambda g, *_: (g, 0)),
                whole(xc.shape),
                block,
            ],
            out_specs=block,
        ),
        compiler_params=pltpu.CompilerParams(vmem_limit_bytes=VMEM_LIMIT),
        cost_estimate=pl.CostEstimate(
            flops=xr.size * xc.shape[0], bytes_accessed=8 * front.size, transcendentals=0
        ),
    )(ids, xr, xc, front)


def column_rows(part, first, local_cols, row_count, col_count, col_dev):
    fold = col_count // row_count
    begin = TILES // col_count
    part = jnp.pad(part, ((0, 0), (first - fold * begin, 0), (0, 0), (0, 0)))
    split = part.reshape(part.shape[0], local_cols - begin, fold, part.shape[2], part.shape[3])
    picked = split[:, :, 0]
    for f in range(1, fold):
        picked = jnp.where(col_dev // row_count == f, split[:, :, f], picked)
    return picked


def from_owner_row(own, row_count, col_count, row_dev, col_dev):
    away = row_dev ^ (col_dev % row_count)
    stride = row_count // 2
    while stride:
        pairs = []
        for r in range(row_count):
            for c in range(col_count):
                if (r ^ (c % row_count)) % (2 * stride) == 0:
                    pairs.append((r * col_count + c, (r ^ stride) * col_count + c))
        arrived = lax.ppermute(own, ("row", "col"), pairs)
        own = jnp.where(away % (2 * stride) == stride, arrived, own)
        stride //= 2
    return own


def gather_columns(panel, b, first, col_count, col_dev, gate):
    rows = panel[first:, b]
    n = rows.shape[0]
    count = min(col_count, TILES - col_count * b)
    if b > 0:
        rows, gate = lax.optimization_barrier((rows, gate))
    if b > 0 and 2 * count == col_count:
        half = (n + 1) // 2
        sent = lax.ppermute(rows[n - half :], "col", [(c, c + count) for c in range(count)])
        both = lax.all_gather(jnp.where(col_dev < count, rows[:half], sent), "col")
        return jnp.concatenate([both[:count], both[count:, 2 * half - n :]], axis=1)
    return lax.all_gather(rows, "col")[:count]


def shards(front_matrix, children, child_map, row_order):
    row_count = lax.axis_size("row")
    col_count = lax.axis_size("col")
    row_dev = lax.axis_index("row")
    col_dev = lax.axis_index("col")
    local_rows = front_matrix.shape[0]
    tile = front_matrix.shape[2]
    local_cols = front_matrix.shape[3]
    lrc = children.shape[1]
    lead_cols = -(-TILES // col_count)
    lead_rows = -(-TILES // row_count)
    first = TILES // row_count
    share = local_rows // col_count
    front = front_matrix.reshape(local_rows * tile * local_cols, tile)
    ids = jnp.stack([row_dev, col_dev]).astype(jnp.int32)

    slots, orders = [], []
    for h in range(2):
        sources, targets, rank = slot_ranks(child_map[h], row_count)
        lands = (child_map[h] // row_count)[:, None] == jnp.arange(local_rows, dtype=jnp.int32)[None, :]
        lands = (lands & (targets == row_dev)[:, None]).astype(jnp.int32)
        slot = sources * (2 * CAP) + h * CAP + rank
        landed = jnp.sum(lands, axis=0)
        slots.append(jnp.where(landed > 0, jnp.sum(lands * slot[:, None], axis=0), -1))
        turned = jnp.sum(lands[:, :, None] * row_order[h][:, None, :], axis=0)
        orders.append(jnp.where((landed > 0)[:, None], turned, -1))
    slots = jnp.stack(slots)
    orders = jnp.stack(orders)

    def exchange(packed):
        arrived = lax.all_to_all(packed, "row", split_axis=0, concat_axis=0, tiled=True)
        return arrived.reshape((row_count * 2 * CAP,) + packed.shape[3:])

    kids = children.reshape(2, lrc, tile, local_cols, tile)
    near = kids[:, :, :, :lead_cols].reshape(2, lrc, tile, lead_cols * tile)
    near = exchange(pack_children(ids, child_map, near, row_count))
    far = pack_children(ids, child_map, kids, row_count)
    near, far = lax.optimization_barrier((near, far))
    fronts = [front_matrix[:, 0, :, b, 0, :] for b in range(lead_cols)]
    high, low = assemble_panel(fronts, orders.transpose(1, 0, 2), jnp.maximum(slots, 0), near)

    places = lead_slots(row_count, col_count, lead_rows, lead_cols)
    lead = jnp.stack([high[a, b].astype(F32) + low[a, b].astype(F32) for a, b in places]).astype(LINK)
    lead = lax.all_gather(lead, "col")
    parts = [gather_columns(high, b, first, col_count, col_dev, lead) for b in range(lead_cols)]
    lead = lax.all_gather(lead, "row")
    lead, far = lax.optimization_barrier((lead, far))
    far = exchange(far)
    blocks = unpack_lead(lead.reshape(-1, tile, tile).astype(F32), row_count, col_count, places)

    diagonals, inverses, inverses_b, lower, lower_b = [], [], [], {}, {}
    sent = []
    for s in range(STEPS):
        if s == STEPS - 1:
            picked = column_rows(parts[0], first, local_cols, row_count, col_count, col_dev)
            blocks[0], picked = lax.optimization_barrier((blocks[0], picked))
            sent.append(from_owner_row(picked, row_count, col_count, row_dev, col_dev))
        c, v, vb = factor_block(blocks[0])
        diagonals.append(c)
        inverses.append(v)
        inverses_b.append(vb)
        left = STEPS - 1 - s
        if left:
            index = lambda t, u: t * (t + 1) // 2 + u
            below = [blocks[index(t, 0)] for t in range(1, left + 1)]
            trail = [blocks[index(t, u)] for t in range(1, left + 1) for u in range(1, t + 1)]
            low_f, low_b, blocks = advance(v, below, trail)
            blocks = list(blocks)
            for n in range(left):
                lower[s + 1 + n, s] = low_f[n]
                lower_b[s + 1 + n, s] = low_b[n]
    inverse = jnp.stack(inverses)
    inverse_b = jnp.stack(inverses_b)
    lower_b = jnp.stack([lower_b[t, u] for t in range(1, STEPS) for u in range(t)])

    joined = join_children(slots, jnp.maximum(orders, 0), far, front, col_count)
    inverse_b, joined = lax.optimization_barrier((inverse_b, joined))
    for p in parts[1:]:
        picked = column_rows(p, first, local_cols, row_count, col_count, col_dev)
        sent.append(from_owner_row(picked, row_count, col_count, row_dev, col_dev))
    xr = solve_rows(parts, first, lower_b, inverse_b)
    xc = solve_rows(sent, TILES // col_count, lower_b, inverse_b)
    schur_part = final_update(ids, xr, xc, joined, row_count, col_count)

    low, parts = lax.optimization_barrier((low, parts))
    rest = low.reshape((col_count, share) + low.shape[1:])
    rest = lax.all_to_all(rest, "col", split_axis=0, concat_axis=0, tiled=True)
    mine = []
    for b, p in enumerate(parts):
        upper = jnp.stack(
            [
                lax.dynamic_index_in_dim(p, jnp.maximum(col_dev * share + k - first, 0), 1, False)
                for k in range(share)
            ],
            axis=1,
        )
        mine.append(upper.astype(F32) + rest[: p.shape[0], :, b].astype(F32))
    nothing = jnp.zeros_like(diagonals[0])
    square = jnp.stack(
        [
            diagonals[t] if t == u else lower[t, u] if u < t else nothing
            for t in range(STEPS)
            for u in range(STEPS)
        ]
    ).reshape((STEPS, STEPS) + nothing.shape)
    factor_part = own_rows(ids, jnp.concatenate(mine, axis=0), square, inverse, row_count)
    return (
        schur_part.reshape(front_matrix.shape),
        factor_part.reshape(share, 1, tile, TILES * tile),
    )


def solution(mesh):
    placed = (
        P(None, "row", None, None, "col", None),
        P(None, None, "row", None, None, "col", None),
        P(),
        P(),
    )
    return jax.shard_map(
        shards,
        mesh=mesh,
        in_specs=placed,
        out_specs=(P(None, "row", None, None, "col", None), P("col", "row", None, None)),
        check_vma=False,
    )
```

```python
import functools

import jax
import jax.numpy as jnp
from jax import lax
from jax.experimental import pallas as pl
from jax.experimental.pallas import tpu as pltpu
from jax.sharding import PartitionSpec as P

PWT = 4
STEPS = 3
CAP = 2
TILES = PWT * STEPS
F32 = jnp.float32
BF16 = jnp.bfloat16
LINK = jnp.float16
VMEM_LIMIT = 60 * 1024 * 1024


def slot_ranks(mapping, row_count):
    indices = jnp.arange(mapping.shape[0], dtype=jnp.int32)
    sources = indices % row_count
    targets = mapping % row_count
    earlier = (
        (sources[:, None] == sources[None, :])
        & (targets[:, None] == targets[None, :])
        & (indices[None, :] < indices[:, None])
    )
    return (sources, targets, jnp.sum(earlier.astype(jnp.int32), axis=1))


def dot(a, b, contract):
    return lax.dot_general(a, b, (contract, ((), ())), preferred_element_type=F32)


NT = ((1,), (1,))
NN = ((1,), (0,))
TN = ((0,), (0,))


def halves(x):
    high = x.astype(BF16)
    return high, (x - high.astype(F32)).astype(BF16)


def dot3(a, b, contract):
    ah, al = halves(a)
    bh, bl = halves(b)
    return dot(ah, bh, contract) + (dot(al, bh, contract) + dot(ah, bl, contract))


def spread_lane(x, j):
    return jnp.broadcast_to(x[:, j : j + 1], (8, x.shape[1]))


def spread_row(x, i):
    return jnp.broadcast_to(x[i : i + 1, :], (8, x.shape[1]))


def factor_tile(tile):
    size = tile.shape[0]
    sub = lax.broadcasted_iota(jnp.int32, (8, size), 0)
    lane = lax.broadcasted_iota(jnp.int32, (8, size), 1)
    groups = size // 8
    left = [tile[8 * s : 8 * s + 8] for s in range(groups)]
    right = [jnp.where(lane == sub + 8 * s, 1.0, 0.0).astype(F32) for s in range(groups)]
    for s in range(groups):
        columns = [spread_lane(left[s], 8 * s + b) for b in range(8)]
        square = {(a, b): spread_row(columns[b], a) for a in range(8) for b in range(a + 1)}
        lrow = [spread_row(left[s], i) for i in range(8)]
        rrow = [spread_row(right[s], i) for i in range(8)]
        more = s + 1 < groups
        ahead = [spread_lane(left[s + 1], 8 * s + b) for b in range(8)] if more else None
        new_left = jnp.zeros((8, size), F32)
        new_right = jnp.zeros((8, size), F32)
        for i in range(8):
            inverse = lax.rsqrt(square[i, i])
            below = {a: square[a, i] * inverse for a in range(i + 1, 8)}
            lrow[i] = lrow[i] * inverse
            rrow[i] = rrow[i] * inverse
            if more:
                ahead[i] = ahead[i] * inverse
            for a in range(i + 1, 8):
                for b in range(i + 1, a + 1):
                    square[a, b] = square[a, b] - below[a] * below[b]
                lrow[a] = lrow[a] - below[a] * lrow[i]
                rrow[a] = rrow[a] - below[a] * rrow[i]
                if more:
                    ahead[a] = ahead[a] - below[a] * ahead[i]
            new_left = jnp.where(sub == i, lrow[i], new_left)
            new_right = jnp.where(sub == i, rrow[i], new_right)
        left[s], right[s] = new_left, new_right
        if more:
            for a in range(8):
                left[s + 1] = left[s + 1] - ahead[a] * lrow[a]
                right[s + 1] = right[s + 1] - ahead[a] * rrow[a]
        if s + 2 < groups:
            both = dot3(new_left, jnp.concatenate([new_left, new_right], 1), TN)
            for t in range(s + 2, groups):
                left[t] = left[t] - both[8 * t : 8 * t + 8, :size]
                right[t] = right[t] - both[8 * t : 8 * t + 8, size:]
    return jnp.concatenate(left, 0), jnp.concatenate(right, 0)


def whole(shape):
    return pl.BlockSpec(shape, lambda *_: (0,) * len(shape), pipeline_mode=pl.Buffered(1))


def pack_kernel(row_count, ids_ref, map_ref, kids_ref, out_ref):
    out_ref[...] = jnp.zeros(out_ref.shape, out_ref.dtype)
    for h in range(2):
        targets = []
        for i in range(kids_ref.shape[1]):
            target = map_ref[h, i * row_count + ids_ref[0]] % row_count
            rank = jnp.int32(0)
            for earlier in targets:
                rank = rank + (earlier == target).astype(jnp.int32)
            targets.append(target)
            out_ref[target, h, rank] = kids_ref[h, i]


def pack_children(ids, child_map, kids, row_count):
    return pl.pallas_call(
        functools.partial(pack_kernel, row_count),
        out_shape=jax.ShapeDtypeStruct((row_count, 2, CAP) + kids.shape[2:], kids.dtype),
        grid_spec=pltpu.PrefetchScalarGridSpec(
            num_scalar_prefetch=2,
            grid=(1,),
            in_specs=[whole(kids.shape)],
            out_specs=whole((row_count, 2, CAP) + kids.shape[2:]),
        ),
        compiler_params=pltpu.CompilerParams(vmem_limit_bytes=VMEM_LIMIT),
    )(ids, child_map, kids)


def panel_kernel(lpc, share, slot_ref, *refs):
    fronts = refs[:lpc]
    order_ref, recv_ref, high_ref, low_ref = refs[lpc:]
    tile = high_ref.shape[-1]
    rows = lax.broadcasted_iota(jnp.int32, (tile, tile), 0)
    for k in range(share):
        a = pl.program_id(0) * share + k
        moved = jnp.zeros((tile, lpc * tile), F32)
        for h in range(2):
            pick = (rows == order_ref[k, h : h + 1, :]).astype(BF16)
            moved = moved + dot(pick, recv_ref[slot_ref[h, a]], NN)
        for b in range(lpc):
            high, low = halves(fronts[b][k] + moved[:, b * tile : (b + 1) * tile])
            high_ref[k, b] = high
            low_ref[k, b] = low


def assemble_panel(fronts, order, slots, received):
    local_rows, tile, _ = fronts[0].shape
    lpc = len(fronts)
    share = 4 if local_rows % 4 == 0 else 1
    out = (local_rows, lpc, tile, tile)
    return pl.pallas_call(
        functools.partial(panel_kernel, lpc, share),
        out_shape=(jax.ShapeDtypeStruct(out, BF16), jax.ShapeDtypeStruct(out, BF16)),
        grid_spec=pltpu.PrefetchScalarGridSpec(
            num_scalar_prefetch=1,
            grid=(local_rows // share,),
            in_specs=[pl.BlockSpec((share, tile, tile), lambda a, s: (a, 0, 0))] * lpc
            + [
                pl.BlockSpec((share, 2, tile), lambda a, s: (a, 0, 0)),
                whole(received.shape),
            ],
            out_specs=[pl.BlockSpec((share,) + out[1:], lambda a, s: (a, 0, 0, 0))] * 2,
        ),
        compiler_params=pltpu.CompilerParams(vmem_limit_bytes=VMEM_LIMIT),
    )(slots, *fronts, order, received)


def lead_slots(row_count, col_count, lead_rows, lead_cols):
    return [
        (a, b)
        for a in range(lead_rows)
        for b in range(lead_cols)
        if col_count * b <= row_count * a + row_count - 1 and col_count * b < TILES
    ]


def unpack_kernel(row_count, col_count, slots, g_ref, *blocks):
    tile = g_ref.shape[-1]
    place = {ab: n for n, ab in enumerate(slots)}
    for i in range(TILES):
        for j in range(i + 1):
            n = place[i // row_count, j // col_count]
            t, u = i // PWT, j // PWT
            rows = pl.ds((i % PWT) * tile, tile)
            cols = pl.ds((j % PWT) * tile, tile)
            source = ((i % row_count) * col_count + j % col_count) * len(slots) + n
            blocks[t * (t + 1) // 2 + u][rows, cols] = g_ref[source]


def unpack_lead(gathered, row_count, col_count, slots):
    width = PWT * gathered.shape[-1]
    count = STEPS * (STEPS + 1) // 2
    return pl.pallas_call(
        functools.partial(unpack_kernel, row_count, col_count, slots),
        out_shape=[jax.ShapeDtypeStruct((width, width), F32)] * count,
        compiler_params=pltpu.CompilerParams(vmem_limit_bytes=VMEM_LIMIT),
    )(gathered)


def block_kernel(d_ref, l_ref, v_ref, vb_ref, work):
    width = d_ref.shape[0]
    tile = width // PWT
    row = lax.broadcasted_iota(jnp.int32, (tile, tile), 0)
    col = lax.broadcasted_iota(jnp.int32, (tile, tile), 1)
    work[...] = d_ref[...]
    l_ref[...] = jnp.zeros((width, width), F32)
    v_ref[...] = jnp.zeros((width, width), F32)
    for k in range(PWT):
        low, high = k * tile, (k + 1) * tile
        block = work[low:high, low:high]
        block = jnp.where(row >= col, block, block.T)
        upper, inverse = factor_tile(block)
        l_ref[low:high, low:high] = jnp.where(row <= col, upper, 0.0).T
        if k > 0:
            v_ref[low:high, 0:low] = dot3(inverse, v_ref[low:high, 0:low], NN)
        v_ref[low:high, low:high] = inverse
        if k < PWT - 1:
            below = dot3(work[high:width, low:high], inverse, NT)
            l_ref[high:width, low:high] = below
            work[high:width, high:width] -= dot3(below, below, NT)
            v_ref[high:width, 0:high] -= dot3(below, v_ref[low:high, 0:high], NN)
    vb_ref[...] = v_ref[...].astype(BF16)


def factor_block(diagonal):
    shape = diagonal.shape
    return pl.pallas_call(
        block_kernel,
        out_shape=(
            jax.ShapeDtypeStruct(shape, F32),
            jax.ShapeDtypeStruct(shape, F32),
            jax.ShapeDtypeStruct(shape, BF16),
        ),
        scratch_shapes=[pltpu.VMEM(shape, F32)],
        compiler_params=pltpu.CompilerParams(vmem_limit_bytes=VMEM_LIMIT),
        cost_estimate=pl.CostEstimate(flops=3 * 10**10, bytes_accessed=4 * 10**6, transcendentals=0),
    )(diagonal)


def advance_kernel(count, v_ref, *refs):
    below, trail = refs[:count], refs[count : count + count * (count + 1) // 2]
    rest = refs[count + len(trail) :]
    lower, lower_b, out = rest[:count], rest[count : 2 * count], rest[2 * count :]
    for t in range(count):
        lower[t][...] = dot3(below[t][...], v_ref[...], NT)
        lower_b[t][...] = lower[t][...].astype(BF16)
    for t in range(count):
        for u in range(t + 1):
            n = t * (t + 1) // 2 + u
            out[n][...] = trail[n][...] - dot3(lower[t][...], lower[u][...], NT)


def advance(inverse, below, trail):
    count = len(below)
    shape = inverse.shape
    kinds = [F32] * count + [BF16] * count + [F32] * len(trail)
    out = pl.pallas_call(
        functools.partial(advance_kernel, count),
        out_shape=[jax.ShapeDtypeStruct(shape, k) for k in kinds],
        compiler_params=pltpu.CompilerParams(vmem_limit_bytes=VMEM_LIMIT),
        cost_estimate=pl.CostEstimate(flops=3 * 10**9, bytes_accessed=10**7, transcendentals=0),
    )(inverse, *below, *trail)
    return out[:count], out[count : 2 * count], out[2 * count :]


def side_by_side(parts):
    return jnp.concatenate([p.reshape(-1, p.shape[-1]) for p in parts], axis=1)


def own_kernel(row_count, ids_ref, own_ref, *refs):
    lower, inverse, out_ref = refs[: STEPS * (STEPS + 1) // 2], refs[-1 - STEPS : -1], refs[-1]
    share, tile = own_ref.shape[1:3]
    width = PWT * tile
    solved = []
    for s in range(STEPS):
        rest = side_by_side([own_ref[s * PWT + j] for j in range(PWT)])
        for q in range(s):
            rest = rest - dot3(solved[q], lower[s * (s + 1) // 2 + q][...], NT)
        solved.append(dot3(rest, inverse[s][...], NT))
        out_ref[:, s * width : (s + 1) * width] = solved[s]
    for k in range(share):
        index = (ids_ref[1] * share + k) * row_count + ids_ref[0]
        for t in range(STEPS):

            @pl.when(index // PWT == t)
            def _(k=k, t=t, index=index):
                source = pl.ds(pl.multiple_of((index % PWT) * tile, tile), tile)
                target = pl.ds(k * tile, tile)
                for s in range(STEPS):
                    if s <= t:
                        value = lower[t * (t + 1) // 2 + s][source, :]
                    else:
                        value = jnp.zeros((tile, width), F32)
                    out_ref[target, s * width : (s + 1) * width] = value


def own_rows(ids, own, lower, inverse, row_count):
    share, tile = own.shape[1:3]
    out = (share * tile, TILES * tile)
    return pl.pallas_call(
        functools.partial(own_kernel, row_count),
        out_shape=jax.ShapeDtypeStruct(out, F32),
        grid_spec=pltpu.PrefetchScalarGridSpec(
            num_scalar_prefetch=1,
            grid=(1,),
            in_specs=[whole(x.shape) for x in (own, *lower, *inverse)],
            out_specs=whole(out),
        ),
        compiler_params=pltpu.CompilerParams(vmem_limit_bytes=VMEM_LIMIT),
        cost_estimate=pl.CostEstimate(flops=6 * 10**9, bytes_accessed=15 * 10**6, transcendentals=0),
    )(ids, own, *lower, *inverse)


def solve_into(parts, lower, inverse, target, first):
    tile = parts[0].shape[-1]
    width = PWT * tile
    count = parts[0].shape[1]
    step = min(4, count)
    where = [(n, j) for n, ref in enumerate(parts) for j in range(ref.shape[0])]
    if first:
        target[0 : first * tile, :] = jnp.zeros((first * tile, target.shape[1]), BF16)

    @pl.loop(0, -(-count // step))
    def _(i):
        a = jnp.minimum(i * step, count - step)
        rows = pl.ds(pl.multiple_of((a + first) * tile, tile), step * tile)
        done = []
        for s in range(STEPS):
            rest = side_by_side([parts[n][j, pl.ds(a, step)] for n, j in where[s * PWT : (s + 1) * PWT]])
            if s > 0:
                rest = rest.astype(F32)
                for q in range(s):
                    rest = rest - dot(done[q], lower[s * (s - 1) // 2 + q][...], NT)
                rest = rest.astype(BF16)
            done.append(dot(rest, inverse[s][...], NT).astype(BF16))
            target[rows, s * width : (s + 1) * width] = done[s]


BELOW = STEPS * (STEPS - 1) // 2


def solve_kernel(first, n_parts, *refs):
    parts, blocks, out_ref = refs[:n_parts], refs[n_parts:-1], refs[-1]
    solve_into(parts, blocks[:BELOW], blocks[BELOW:], out_ref, first)


def solve_rows(parts, first, lower, inverse):
    tile = parts[0].shape[-1]
    count = parts[0].shape[1]
    rows = (first + count) * tile
    return pl.pallas_call(
        functools.partial(solve_kernel, first, len(parts)),
        out_shape=jax.ShapeDtypeStruct((rows, TILES * tile), BF16),
        compiler_params=pltpu.CompilerParams(vmem_limit_bytes=VMEM_LIMIT),
        cost_estimate=pl.CostEstimate(
            flops=count * tile * (TILES * tile) ** 2 * 2,
            bytes_accessed=4 * rows * TILES * tile,
            transcendentals=0,
        ),
    )(*parts, *lower, *inverse)


def final_kernel(row_count, col_count, n_parts, ids_ref, slot_ref, order_ref, *refs):
    parts, blocks = refs[:n_parts], refs[n_parts : n_parts + BELOW + STEPS]
    recv_ref, xr_ref, front_ref, out_ref, xc_ref = refs[n_parts + BELOW + STEPS :]
    g = pl.program_id(0)
    tile = out_ref.shape[-1]
    share = xr_ref.shape[0] // tile
    local_cols = xc_ref.shape[0] // tile

    @pl.when(g == 0)
    def _():
        solve_into(parts, blocks[:BELOW], blocks[BELOW:], xc_ref, local_cols - parts[0].shape[1])

    out_ref[...] = front_ref[...]
    for k in range(share):
        a = g * share + k
        for h in range(2):
            slot = slot_ref[h, a]

            @pl.when(slot >= 0)
            def _(a=a, k=k, h=h, slot=slot):
                @pl.loop(0, tile, unroll=8)
                def _(t):
                    at = (k * tile + order_ref[h, a, t]) * local_cols
                    at = pl.ds(pl.multiple_of(at, local_cols), local_cols)
                    out_ref[at, :] += recv_ref[slot, t].astype(F32)

    last = row_count * (g * share + share - 1) + ids_ref[0]
    pair = 2 if local_cols % 2 == 0 else 1
    for b in range(0, local_cols, pair):
        some = last >= jnp.maximum(col_count * b + ids_ref[1], TILES)

        @pl.when(some)
        def _(b=b):
            update = dot(xr_ref[...], xc_ref[b * tile : (b + pair) * tile, :], NT)
            for k in range(share):
                row_tile = row_count * (g * share + k) + ids_ref[0]
                for j in range(pair):
                    col_tile = col_count * (b + j) + ids_ref[1]
                    keep = (row_tile >= col_tile) & (col_tile >= TILES)
                    at = pl.ds(k * tile * local_cols + b + j, tile, stride=local_cols)
                    part = update[k * tile : (k + 1) * tile, j * tile : (j + 1) * tile]
                    out_ref[at, :] = jnp.where(keep, out_ref[at, :] - part, 0.0)

        @pl.when(jnp.logical_not(some))
        def _(b=b):
            for j in range(pair):
                out_ref[pl.ds(b + j, share * tile, stride=local_cols), :] = jnp.zeros(
                    (share * tile, tile), F32
                )


def final_update(ids, slots, order, parts, lower, inverse, received, xr, front, row_count, col_count):
    rows = front.shape[0] // col_count
    block = pl.BlockSpec((rows, front.shape[1]), lambda g, *_: (g, 0))
    held = (*parts, *lower, *inverse, received)
    return pl.pallas_call(
        functools.partial(final_kernel, row_count, col_count, len(parts)),
        out_shape=jax.ShapeDtypeStruct(front.shape, F32),
        grid_spec=pltpu.PrefetchScalarGridSpec(
            num_scalar_prefetch=3,
            grid=(col_count,),
            in_specs=[whole(x.shape) for x in held]
            + [pl.BlockSpec((xr.shape[0] // col_count, xr.shape[1]), lambda g, *_: (g, 0)), block],
            out_specs=block,
            scratch_shapes=[pltpu.VMEM((received.shape[2] * front.shape[1], xr.shape[1]), BF16)],
        ),
        compiler_params=pltpu.CompilerParams(vmem_limit_bytes=VMEM_LIMIT),
        cost_estimate=pl.CostEstimate(
            flops=2 * xr.size * xr.shape[1], bytes_accessed=8 * front.size, transcendentals=0
        ),
    )(ids, slots, order, *held, xr, front)


def column_rows(part, first, local_cols, row_count, col_count, col_dev):
    fold = col_count // row_count
    begin = TILES // col_count
    part = jnp.pad(part, ((0, 0), (first - fold * begin, 0), (0, 0), (0, 0)))
    split = part.reshape(part.shape[0], local_cols - begin, fold, part.shape[2], part.shape[3])
    picked = split[:, :, 0]
    for f in range(1, fold):
        picked = jnp.where(col_dev // row_count == f, split[:, :, f], picked)
    return picked


def from_owner_row(own, row_count, col_count, row_dev, col_dev):
    away = row_dev ^ (col_dev % row_count)
    stride = row_count // 2
    while stride:
        pairs = []
        for r in range(row_count):
            for c in range(col_count):
                if (r ^ (c % row_count)) % (2 * stride) == 0:
                    pairs.append((r * col_count + c, (r ^ stride) * col_count + c))
        arrived = lax.ppermute(own, ("row", "col"), pairs)
        own = jnp.where(away % (2 * stride) == stride, arrived, own)
        stride //= 2
    return own


def gather_columns(panel, b, first, col_count, col_dev):
    rows = panel[first:, b]
    n = rows.shape[0]
    count = min(col_count, TILES - col_count * b)
    if b > 0 and 2 * count == col_count:
        half = (n + 1) // 2
        sent = lax.ppermute(rows[n - half :], "col", [(c, c + count) for c in range(count)])
        rows = jnp.where(col_dev < count, rows[:half], sent)
    return lax.all_gather(rows, "col")


def merge_columns(gathered, b, n, col_count):
    count = min(col_count, TILES - col_count * b)
    half = gathered.shape[1]
    if half < n:
        return jnp.concatenate([gathered[:count], gathered[count:, 2 * half - n :]], axis=1)
    return gathered[:count]


def shards(front_matrix, children, child_map, row_order):
    row_count = lax.axis_size("row")
    col_count = lax.axis_size("col")
    row_dev = lax.axis_index("row")
    col_dev = lax.axis_index("col")
    local_rows = front_matrix.shape[0]
    tile = front_matrix.shape[2]
    local_cols = front_matrix.shape[3]
    lrc = children.shape[1]
    lead_cols = -(-TILES // col_count)
    lead_rows = -(-TILES // row_count)
    first = TILES // row_count
    share = local_rows // col_count
    front = front_matrix.reshape(local_rows * tile * local_cols, tile)
    ids = jnp.stack([row_dev, col_dev]).astype(jnp.int32)

    slots, orders = [], []
    for h in range(2):
        sources, targets, rank = slot_ranks(child_map[h], row_count)
        lands = (child_map[h] // row_count)[:, None] == jnp.arange(local_rows, dtype=jnp.int32)[None, :]
        lands = (lands & (targets == row_dev)[:, None]).astype(jnp.int32)
        slot = sources * (2 * CAP) + h * CAP + rank
        landed = jnp.sum(lands, axis=0)
        slots.append(jnp.where(landed > 0, jnp.sum(lands * slot[:, None], axis=0), -1))
        turned = jnp.sum(lands[:, :, None] * row_order[h][:, None, :], axis=0)
        orders.append(jnp.where((landed > 0)[:, None], turned, -1))
    slots = jnp.stack(slots)
    orders = jnp.stack(orders)

    def exchange(packed):
        arrived = lax.all_to_all(packed, "row", split_axis=0, concat_axis=0, tiled=True)
        return arrived.reshape((row_count * 2 * CAP,) + packed.shape[3:])

    kids = children.reshape(2, lrc, tile, local_cols, tile)
    near = kids[:, :, :, :lead_cols].reshape(2, lrc, tile, lead_cols * tile)
    near = exchange(pack_children(ids, child_map, near, row_count))
    far = pack_children(ids, child_map, kids, row_count)
    near, far = lax.optimization_barrier((near, far))
    fronts = [front_matrix[:, 0, :, b, 0, :] for b in range(lead_cols)]
    high, low = assemble_panel(fronts, orders.transpose(1, 0, 2), jnp.maximum(slots, 0), near)

    places = lead_slots(row_count, col_count, lead_rows, lead_cols)
    lead = jnp.stack([high[a, b].astype(F32) + low[a, b].astype(F32) for a, b in places]).astype(LINK)
    lead = lax.all_gather(lead, "col")
    height = local_rows - first
    parts = [merge_columns(gather_columns(high, 0, first, col_count, col_dev), 0, height, col_count)]
    lead = lax.all_gather(lead, "row")
    lead, far = lax.optimization_barrier((lead, far))
    far = exchange(far)
    blocks = unpack_lead(lead.reshape(-1, tile, tile).astype(F32), row_count, col_count, places)

    diagonals, inverses, inverses_b, lower, lower_b = [], [], [], {}, {}
    sent = []
    for s in range(STEPS):
        if s == STEPS - 1:
            picked = column_rows(parts[0], first, local_cols, row_count, col_count, col_dev)
            blocks[0], picked, far = lax.optimization_barrier((blocks[0], picked, far))
            sent.append(from_owner_row(picked, row_count, col_count, row_dev, col_dev))
        c, v, vb = factor_block(blocks[0])
        diagonals.append(c)
        inverses.append(v)
        inverses_b.append(vb)
        if s == 0 and lead_cols > 1:
            later, _ = lax.optimization_barrier((high, vb))
            late = gather_columns(later, lead_cols - 1, first, col_count, col_dev)
        left = STEPS - 1 - s
        if left:
            index = lambda t, u: t * (t + 1) // 2 + u
            below = [blocks[index(t, 0)] for t in range(1, left + 1)]
            trail = [blocks[index(t, u)] for t in range(1, left + 1) for u in range(1, t + 1)]
            low_f, low_b, blocks = advance(v, below, trail)
            blocks = list(blocks)
            for n in range(left):
                lower[s + 1 + n, s] = low_f[n]
                lower_b[s + 1 + n, s] = low_b[n]
    triangle = [
        diagonals[t] if t == u else lower[t, u] for t in range(STEPS) for u in range(t + 1)
    ]
    below_b = [lower_b[t, u] for t in range(1, STEPS) for u in range(t)]

    if lead_cols > 1:
        late, inverses_b[-1] = lax.optimization_barrier((late, inverses_b[-1]))
        parts.append(merge_columns(late, lead_cols - 1, height, col_count))
        picked = column_rows(parts[-1], first, local_cols, row_count, col_count, col_dev)
        inverses_b[-1], picked = lax.optimization_barrier((inverses_b[-1], picked))
        sent.append(from_owner_row(picked, row_count, col_count, row_dev, col_dev))
    xr = solve_rows(parts, first, below_b, inverses_b)
    schur_part = final_update(
        ids, slots, jnp.maximum(orders, 0), sent, below_b, inverses_b, far, xr, front, row_count, col_count
    )

    low, parts = lax.optimization_barrier((low, parts))
    rest = low.reshape((col_count, share) + low.shape[1:])
    rest = lax.all_to_all(rest, "col", split_axis=0, concat_axis=0, tiled=True)
    mine = []
    for b, p in enumerate(parts):
        upper = jnp.stack(
            [
                lax.dynamic_index_in_dim(p, jnp.maximum(col_dev * share + k - first, 0), 1, False)
                for k in range(share)
            ],
            axis=1,
        )
        mine.append(upper.astype(F32) + rest[: p.shape[0], :, b].astype(F32))
    factor_part = own_rows(ids, jnp.concatenate(mine, axis=0), triangle, inverses, row_count)

    return (
        schur_part.reshape(front_matrix.shape),
        factor_part.reshape(share, 1, tile, TILES * tile),
    )


def solution(mesh):
    placed = (
        P(None, "row", None, None, "col", None),
        P(None, None, "row", None, None, "col", None),
        P(),
        P(),
    )
    return jax.shard_map(
        shards,
        mesh=mesh,
        in_specs=placed,
        out_specs=(P(None, "row", None, None, "col", None), P("col", "row", None, None)),
        check_vma=False,
    )
```

```python
import functools

import jax
import jax.numpy as jnp
from jax import lax
from jax.experimental import pallas as pl
from jax.experimental.pallas import tpu as pltpu
from jax.sharding import PartitionSpec as P

PWT = 4
STEPS = 3
CAP = 2
TILES = PWT * STEPS
F32 = jnp.float32
BF16 = jnp.bfloat16
LINK = jnp.float16
VMEM_LIMIT = 60 * 1024 * 1024


def slot_ranks(mapping, row_count):
    indices = jnp.arange(mapping.shape[0], dtype=jnp.int32)
    sources = indices % row_count
    targets = mapping % row_count
    earlier = (
        (sources[:, None] == sources[None, :])
        & (targets[:, None] == targets[None, :])
        & (indices[None, :] < indices[:, None])
    )
    return (sources, targets, jnp.sum(earlier.astype(jnp.int32), axis=1))


def dot(a, b, contract):
    return lax.dot_general(a, b, (contract, ((), ())), preferred_element_type=F32)


NT = ((1,), (1,))
NN = ((1,), (0,))
TN = ((0,), (0,))


def halves(x):
    high = x.astype(BF16)
    return high, (x - high.astype(F32)).astype(BF16)


def dot3(a, b, contract):
    ah, al = halves(a)
    bh, bl = halves(b)
    return dot(ah, bh, contract) + (dot(al, bh, contract) + dot(ah, bl, contract))


def spread_lane(x, j):
    return jnp.broadcast_to(x[:, j : j + 1], (8, x.shape[1]))


def spread_row(x, i):
    return jnp.broadcast_to(x[i : i + 1, :], (8, x.shape[1]))


def factor_tile(tile):
    size = tile.shape[0]
    sub = lax.broadcasted_iota(jnp.int32, (8, size), 0)
    lane = lax.broadcasted_iota(jnp.int32, (8, size), 1)
    groups = size // 8
    left = [tile[8 * s : 8 * s + 8] for s in range(groups)]
    right = [jnp.where(lane == sub + 8 * s, 1.0, 0.0).astype(F32) for s in range(groups)]
    for s in range(groups):
        columns = [spread_lane(left[s], 8 * s + b) for b in range(8)]
        square = {(a, b): spread_row(columns[b], a) for a in range(8) for b in range(a + 1)}
        lrow = [spread_row(left[s], i) for i in range(8)]
        rrow = [spread_row(right[s], i) for i in range(8)]
        more = s + 1 < groups
        ahead = [spread_lane(left[s + 1], 8 * s + b) for b in range(8)] if more else None
        new_left = jnp.zeros((8, size), F32)
        new_right = jnp.zeros((8, size), F32)
        for i in range(8):
            inverse = lax.rsqrt(square[i, i])
            below = {a: square[a, i] * inverse for a in range(i + 1, 8)}
            lrow[i] = lrow[i] * inverse
            rrow[i] = rrow[i] * inverse
            if more:
                ahead[i] = ahead[i] * inverse
            for a in range(i + 1, 8):
                for b in range(i + 1, a + 1):
                    square[a, b] = square[a, b] - below[a] * below[b]
                lrow[a] = lrow[a] - below[a] * lrow[i]
                rrow[a] = rrow[a] - below[a] * rrow[i]
                if more:
                    ahead[a] = ahead[a] - below[a] * ahead[i]
            new_left = jnp.where(sub == i, lrow[i], new_left)
            new_right = jnp.where(sub == i, rrow[i], new_right)
        left[s], right[s] = new_left, new_right
        if more:
            for a in range(8):
                left[s + 1] = left[s + 1] - ahead[a] * lrow[a]
                right[s + 1] = right[s + 1] - ahead[a] * rrow[a]
        if s + 2 < groups:
            both = dot3(new_left, jnp.concatenate([new_left, new_right], 1), TN)
            for t in range(s + 2, groups):
                left[t] = left[t] - both[8 * t : 8 * t + 8, :size]
                right[t] = right[t] - both[8 * t : 8 * t + 8, size:]
    return jnp.concatenate(left, 0), jnp.concatenate(right, 0)


def whole(shape):
    return pl.BlockSpec(shape, lambda *_: (0,) * len(shape), pipeline_mode=pl.Buffered(1))


def pack_kernel(row_count, ids_ref, map_ref, kids_ref, out_ref):
    out_ref[...] = jnp.zeros(out_ref.shape, out_ref.dtype)
    for h in range(2):
        targets = []
        for i in range(kids_ref.shape[1]):
            target = map_ref[h, i * row_count + ids_ref[0]] % row_count
            rank = jnp.int32(0)
            for earlier in targets:
                rank = rank + (earlier == target).astype(jnp.int32)
            targets.append(target)
            out_ref[target, h, rank] = kids_ref[h, i]


def pack_children(ids, child_map, kids, row_count):
    return pl.pallas_call(
        functools.partial(pack_kernel, row_count),
        out_shape=jax.ShapeDtypeStruct((row_count, 2, CAP) + kids.shape[2:], kids.dtype),
        grid_spec=pltpu.PrefetchScalarGridSpec(
            num_scalar_prefetch=2,
            grid=(1,),
            in_specs=[whole(kids.shape)],
            out_specs=whole((row_count, 2, CAP) + kids.shape[2:]),
        ),
        compiler_params=pltpu.CompilerParams(vmem_limit_bytes=VMEM_LIMIT),
    )(ids, child_map, kids)


def panel_kernel(lpc, share, slot_ref, *refs):
    fronts = refs[:lpc]
    order_ref, recv_ref, high_ref, low_ref = refs[lpc:]
    tile = high_ref.shape[-1]
    rows = lax.broadcasted_iota(jnp.int32, (tile, tile), 0)
    for k in range(share):
        a = pl.program_id(0) * share + k
        moved = jnp.zeros((tile, lpc * tile), F32)
        for h in range(2):
            pick = (rows == order_ref[k, h : h + 1, :]).astype(BF16)
            moved = moved + dot(pick, recv_ref[slot_ref[h, a]], NN)
        for b in range(lpc):
            high, low = halves(fronts[b][k] + moved[:, b * tile : (b + 1) * tile])
            high_ref[k, b] = high
            low_ref[k, b] = low


def assemble_panel(fronts, order, slots, received):
    local_rows, tile, _ = fronts[0].shape
    lpc = len(fronts)
    share = 4 if local_rows % 4 == 0 else 1
    out = (local_rows, lpc, tile, tile)
    return pl.pallas_call(
        functools.partial(panel_kernel, lpc, share),
        out_shape=(jax.ShapeDtypeStruct(out, BF16), jax.ShapeDtypeStruct(out, BF16)),
        grid_spec=pltpu.PrefetchScalarGridSpec(
            num_scalar_prefetch=1,
            grid=(local_rows // share,),
            in_specs=[pl.BlockSpec((share, tile, tile), lambda a, s: (a, 0, 0))] * lpc
            + [
                pl.BlockSpec((share, 2, tile), lambda a, s: (a, 0, 0)),
                whole(received.shape),
            ],
            out_specs=[pl.BlockSpec((share,) + out[1:], lambda a, s: (a, 0, 0, 0))] * 2,
        ),
        compiler_params=pltpu.CompilerParams(vmem_limit_bytes=VMEM_LIMIT),
    )(slots, *fronts, order, received)


def lead_slots(row_count, col_count, lead_rows, lead_cols):
    return [
        (a, b)
        for a in range(lead_rows)
        for b in range(lead_cols)
        if col_count * b <= row_count * a + row_count - 1 and col_count * b < TILES
    ]


def unpack_kernel(row_count, col_count, slots, g_ref, *blocks):
    tile = g_ref.shape[-1]
    place = {ab: n for n, ab in enumerate(slots)}
    for i in range(TILES):
        for j in range(i + 1):
            n = place[i // row_count, j // col_count]
            t, u = i // PWT, j // PWT
            rows = pl.ds((i % PWT) * tile, tile)
            cols = pl.ds((j % PWT) * tile, tile)
            source = ((i % row_count) * col_count + j % col_count) * len(slots) + n
            blocks[t * (t + 1) // 2 + u][rows, cols] = g_ref[source]


def unpack_lead(gathered, row_count, col_count, slots):
    width = PWT * gathered.shape[-1]
    count = STEPS * (STEPS + 1) // 2
    return pl.pallas_call(
        functools.partial(unpack_kernel, row_count, col_count, slots),
        out_shape=[jax.ShapeDtypeStruct((width, width), F32)] * count,
        compiler_params=pltpu.CompilerParams(vmem_limit_bytes=VMEM_LIMIT),
    )(gathered)


def block_kernel(d_ref, l_ref, v_ref, vb_ref, work):
    width = d_ref.shape[0]
    tile = width // PWT
    row = lax.broadcasted_iota(jnp.int32, (tile, tile), 0)
    col = lax.broadcasted_iota(jnp.int32, (tile, tile), 1)
    work[...] = d_ref[...]
    l_ref[...] = jnp.zeros((width, width), F32)
    v_ref[...] = jnp.zeros((width, width), F32)
    for k in range(PWT):
        low, high = k * tile, (k + 1) * tile
        block = work[low:high, low:high]
        block = jnp.where(row >= col, block, block.T)
        upper, inverse = factor_tile(block)
        l_ref[low:high, low:high] = jnp.where(row <= col, upper, 0.0).T
        if k > 0:
            v_ref[low:high, 0:low] = dot3(inverse, v_ref[low:high, 0:low], NN)
        v_ref[low:high, low:high] = inverse
        if k < PWT - 1:
            below = dot3(work[high:width, low:high], inverse, NT)
            l_ref[high:width, low:high] = below
            work[high:width, high:width] -= dot3(below, below, NT)
            v_ref[high:width, 0:high] -= dot3(below, v_ref[low:high, 0:high], NN)
    vb_ref[...] = v_ref[...].astype(BF16)


def factor_block(diagonal):
    shape = diagonal.shape
    return pl.pallas_call(
        block_kernel,
        out_shape=(
            jax.ShapeDtypeStruct(shape, F32),
            jax.ShapeDtypeStruct(shape, F32),
            jax.ShapeDtypeStruct(shape, BF16),
        ),
        scratch_shapes=[pltpu.VMEM(shape, F32)],
        compiler_params=pltpu.CompilerParams(vmem_limit_bytes=VMEM_LIMIT),
        cost_estimate=pl.CostEstimate(flops=3 * 10**10, bytes_accessed=4 * 10**6, transcendentals=0),
    )(diagonal)


def advance_kernel(count, v_ref, *refs):
    below, trail = refs[:count], refs[count : count + count * (count + 1) // 2]
    rest = refs[count + len(trail) :]
    lower, lower_b, out = rest[:count], rest[count : 2 * count], rest[2 * count :]
    for t in range(count):
        lower[t][...] = dot3(below[t][...], v_ref[...], NT)
        lower_b[t][...] = lower[t][...].astype(BF16)
    for t in range(count):
        for u in range(t + 1):
            n = t * (t + 1) // 2 + u
            out[n][...] = trail[n][...] - dot3(lower[t][...], lower[u][...], NT)


def advance(inverse, below, trail):
    count = len(below)
    shape = inverse.shape
    kinds = [F32] * count + [BF16] * count + [F32] * len(trail)
    out = pl.pallas_call(
        functools.partial(advance_kernel, count),
        out_shape=[jax.ShapeDtypeStruct(shape, k) for k in kinds],
        compiler_params=pltpu.CompilerParams(vmem_limit_bytes=VMEM_LIMIT),
        cost_estimate=pl.CostEstimate(flops=3 * 10**9, bytes_accessed=10**7, transcendentals=0),
    )(inverse, *below, *trail)
    return out[:count], out[count : 2 * count], out[2 * count :]


def side_by_side(parts):
    return jnp.concatenate([p.reshape(-1, p.shape[-1]) for p in parts], axis=1)


def own_kernel(row_count, ids_ref, own_ref, *refs):
    lower, inverse, out_ref = refs[: STEPS * (STEPS + 1) // 2], refs[-1 - STEPS : -1], refs[-1]
    share, tile = own_ref.shape[1:3]
    width = PWT * tile
    solved = []
    for s in range(STEPS):
        rest = side_by_side([own_ref[s * PWT + j] for j in range(PWT)])
        for q in range(s):
            rest = rest - dot3(solved[q], lower[s * (s + 1) // 2 + q][...], NT)
        solved.append(dot3(rest, inverse[s][...], NT))
        out_ref[:, s * width : (s + 1) * width] = solved[s]
    for k in range(share):
        index = (ids_ref[1] * share + k) * row_count + ids_ref[0]
        for t in range(STEPS):

            @pl.when(index // PWT == t)
            def _(k=k, t=t, index=index):
                source = pl.ds(pl.multiple_of((index % PWT) * tile, tile), tile)
                target = pl.ds(k * tile, tile)
                for s in range(STEPS):
                    if s <= t:
                        value = lower[t * (t + 1) // 2 + s][source, :]
                    else:
                        value = jnp.zeros((tile, width), F32)
                    out_ref[target, s * width : (s + 1) * width] = value


def own_rows(ids, own, lower, inverse, row_count):
    share, tile = own.shape[1:3]
    out = (share * tile, TILES * tile)
    return pl.pallas_call(
        functools.partial(own_kernel, row_count),
        out_shape=jax.ShapeDtypeStruct(out, F32),
        grid_spec=pltpu.PrefetchScalarGridSpec(
            num_scalar_prefetch=1,
            grid=(1,),
            in_specs=[whole(x.shape) for x in (own, *lower, *inverse)],
            out_specs=whole(out),
        ),
        compiler_params=pltpu.CompilerParams(vmem_limit_bytes=VMEM_LIMIT),
        cost_estimate=pl.CostEstimate(flops=6 * 10**9, bytes_accessed=15 * 10**6, transcendentals=0),
    )(ids, own, *lower, *inverse)


def solve_into(parts, lower, inverse, target, first):
    tile = parts[0].shape[-1]
    width = PWT * tile
    count = parts[0].shape[1]
    step = min(4, count)
    where = [(n, j) for n, ref in enumerate(parts) for j in range(ref.shape[0])]
    if first:
        target[0 : first * tile, :] = jnp.zeros((first * tile, target.shape[1]), BF16)

    @pl.loop(0, -(-count // step))
    def _(i):
        a = jnp.minimum(i * step, count - step)
        rows = pl.ds(pl.multiple_of((a + first) * tile, tile), step * tile)
        done = []
        for s in range(STEPS):
            rest = side_by_side([parts[n][j, pl.ds(a, step)] for n, j in where[s * PWT : (s + 1) * PWT]])
            if s > 0:
                rest = rest.astype(F32)
                for q in range(s):
                    rest = rest - dot(done[q], lower[s * (s - 1) // 2 + q][...], NT)
                rest = rest.astype(BF16)
            done.append(dot(rest, inverse[s][...], NT).astype(BF16))
            target[rows, s * width : (s + 1) * width] = done[s]


BELOW = STEPS * (STEPS - 1) // 2


def solve_kernel(begin, end, step, *refs):
    row_refs, refs = refs[:step], refs[step:]
    known, blocks, out_ref = refs[: min(begin, 1)], refs[min(begin, 1) : -1], refs[-1]
    lower, inverse = blocks[:BELOW], blocks[BELOW:]
    width = PWT * row_refs[0].shape[-1]
    done = [known[0][:, q * width : (q + 1) * width] for q in range(begin)]
    for s in range(begin, end):
        columns = range((s - begin) * PWT, (s - begin + 1) * PWT)
        rest = jnp.concatenate([side_by_side([ref[j] for j in columns]) for ref in row_refs], axis=0)
        if s > 0:
            rest = rest.astype(F32)
            for q in range(s):
                rest = rest - dot(done[q], lower[s * (s - 1) // 2 + q][...], NT)
            rest = rest.astype(BF16)
        done.append(dot(rest, inverse[s][...], NT).astype(BF16))
        out_ref[:, (s - begin) * width : (s - begin + 1) * width] = done[s]


def solve_rows(part, known, begin, lower, inverse):
    tile = part.shape[-1]
    step = 4
    steps = -(-part.shape[1] // step)
    end = begin + part.shape[0] // PWT
    width = PWT * tile
    rows = step * tile
    known = [known] if begin else []
    held = (*lower, *inverse)

    def row_tile(k):
        last = part.shape[1] - 1
        return pl.BlockSpec(
            (part.shape[0], 1, tile, tile), lambda i: (0, jnp.minimum(i * step + k, last), 0, 0)
        )

    return pl.pallas_call(
        functools.partial(solve_kernel, begin, end, step),
        out_shape=jax.ShapeDtypeStruct((steps * rows, (end - begin) * width), BF16),
        grid=(steps,),
        in_specs=[row_tile(k) for k in range(step)]
        + [pl.BlockSpec((rows, k.shape[1]), lambda i: (i, 0)) for k in known]
        + [whole(x.shape) for x in held],
        out_specs=pl.BlockSpec((rows, (end - begin) * width), lambda i: (i, 0)),
        compiler_params=pltpu.CompilerParams(vmem_limit_bytes=VMEM_LIMIT),
        cost_estimate=pl.CostEstimate(
            flops=2 * steps * rows * (end - begin) * width * end * width,
            bytes_accessed=4 * part.size,
            transcendentals=0,
        ),
    )(*[part] * step, *known, *held)


def final_kernel(row_count, col_count, n_parts, ids_ref, slot_ref, order_ref, *refs):
    parts, blocks = refs[:n_parts], refs[n_parts : n_parts + BELOW + STEPS]
    rest = refs[n_parts + BELOW + STEPS :]
    recv_ref, row_refs, (front_ref, out_ref, xc_ref, xr_ref) = rest[0], rest[1:-4], rest[-4:]
    g = pl.program_id(0)
    tile = out_ref.shape[-1]
    share = xr_ref.shape[0] // tile
    for n, ref in enumerate(row_refs):
        k = n % share
        left = 0 if n < share else row_refs[0].shape[1]
        xr_ref[k * tile : (k + 1) * tile, left : left + ref.shape[1]] = ref[...]
    local_cols = xc_ref.shape[0] // tile

    @pl.when(g == 0)
    def _():
        solve_into(parts, blocks[:BELOW], blocks[BELOW:], xc_ref, local_cols - parts[0].shape[1])

    out_ref[...] = front_ref[...]
    for k in range(share):
        a = g * share + k
        for h in range(2):
            slot = slot_ref[h, a]

            @pl.when(slot >= 0)
            def _(a=a, k=k, h=h, slot=slot):
                @pl.loop(0, tile, unroll=8)
                def _(t):
                    at = (k * tile + order_ref[h, a, t]) * local_cols
                    at = pl.ds(pl.multiple_of(at, local_cols), local_cols)
                    out_ref[at, :] += recv_ref[slot, t].astype(F32)

    last = row_count * (g * share + share - 1) + ids_ref[0]
    pair = 2 if local_cols % 2 == 0 else 1
    for b in range(0, local_cols, pair):
        some = last >= jnp.maximum(col_count * b + ids_ref[1], TILES)

        @pl.when(some)
        def _(b=b):
            update = dot(xr_ref[...], xc_ref[b * tile : (b + pair) * tile, :], NT)
            for k in range(share):
                row_tile = row_count * (g * share + k) + ids_ref[0]
                for j in range(pair):
                    col_tile = col_count * (b + j) + ids_ref[1]
                    keep = (row_tile >= col_tile) & (col_tile >= TILES)
                    at = pl.ds(k * tile * local_cols + b + j, tile, stride=local_cols)
                    part = update[k * tile : (k + 1) * tile, j * tile : (j + 1) * tile]
                    out_ref[at, :] = jnp.where(keep, out_ref[at, :] - part, 0.0)

        @pl.when(jnp.logical_not(some))
        def _(b=b):
            for j in range(pair):
                out_ref[pl.ds(b + j, share * tile, stride=local_cols), :] = jnp.zeros(
                    (share * tile, tile), F32
                )


def final_update(
    ids, slots, order, parts, lower, inverse, received, solved, first, front, row_count, col_count
):
    rows = front.shape[0] // col_count
    tile = front.shape[1]
    share = slots.shape[1] // col_count
    wide = sum(x.shape[1] for x in solved)
    block = pl.BlockSpec((rows, tile), lambda g, *_: (g, 0))
    held = (*parts, *lower, *inverse, received)

    def row_tile(k, x):
        return pl.BlockSpec(
            (tile, x.shape[1]), lambda g, *_: (jnp.maximum(g * share + k - first, 0), 0)
        )

    return pl.pallas_call(
        functools.partial(final_kernel, row_count, col_count, len(parts)),
        out_shape=jax.ShapeDtypeStruct(front.shape, F32),
        grid_spec=pltpu.PrefetchScalarGridSpec(
            num_scalar_prefetch=3,
            grid=(col_count,),
            in_specs=[whole(x.shape) for x in held]
            + [row_tile(k, x) for x in solved for k in range(share)]
            + [block],
            out_specs=block,
            scratch_shapes=[
                pltpu.VMEM((received.shape[2] * tile, wide), BF16),
                pltpu.VMEM((share * tile, wide), BF16),
            ],
        ),
        compiler_params=pltpu.CompilerParams(vmem_limit_bytes=VMEM_LIMIT),
        cost_estimate=pl.CostEstimate(
            flops=2 * slots.shape[1] * tile * wide * wide, bytes_accessed=8 * front.size, transcendentals=0
        ),
    )(ids, slots, order, *held, *[x for x in solved for _ in range(share)], front)


def column_rows(part, first, local_cols, row_count, col_count, col_dev):
    fold = col_count // row_count
    begin = TILES // col_count
    part = jnp.pad(part, ((0, 0), (first - fold * begin, 0), (0, 0), (0, 0)))
    split = part.reshape(part.shape[0], local_cols - begin, fold, part.shape[2], part.shape[3])
    picked = split[:, :, 0]
    for f in range(1, fold):
        picked = jnp.where(col_dev // row_count == f, split[:, :, f], picked)
    return picked


def from_owner_row(own, row_count, col_count, row_dev, col_dev):
    away = row_dev ^ (col_dev % row_count)
    stride = row_count // 2
    while stride:
        pairs = []
        for r in range(row_count):
            for c in range(col_count):
                if (r ^ (c % row_count)) % (2 * stride) == 0:
                    pairs.append((r * col_count + c, (r ^ stride) * col_count + c))
        arrived = lax.ppermute(own, ("row", "col"), pairs)
        own = jnp.where(away % (2 * stride) == stride, arrived, own)
        stride //= 2
    return own


def gather_columns(panel, b, first, col_count, col_dev):
    rows = panel[first:, b]
    n = rows.shape[0]
    count = min(col_count, TILES - col_count * b)
    if b > 0 and 2 * count == col_count:
        half = (n + 1) // 2
        sent = lax.ppermute(rows[n - half :], "col", [(c, c + count) for c in range(count)])
        rows = jnp.where(col_dev < count, rows[:half], sent)
    return lax.all_gather(rows, "col")


def merge_columns(gathered, b, n, col_count):
    count = min(col_count, TILES - col_count * b)
    half = gathered.shape[1]
    if half < n:
        return jnp.concatenate([gathered[:count], gathered[count:, 2 * half - n :]], axis=1)
    return gathered[:count]


def shards(front_matrix, children, child_map, row_order):
    row_count = lax.axis_size("row")
    col_count = lax.axis_size("col")
    row_dev = lax.axis_index("row")
    col_dev = lax.axis_index("col")
    local_rows = front_matrix.shape[0]
    tile = front_matrix.shape[2]
    local_cols = front_matrix.shape[3]
    lrc = children.shape[1]
    lead_cols = -(-TILES // col_count)
    lead_rows = -(-TILES // row_count)
    first = TILES // row_count
    share = local_rows // col_count
    front = front_matrix.reshape(local_rows * tile * local_cols, tile)
    ids = jnp.stack([row_dev, col_dev]).astype(jnp.int32)

    slots, orders = [], []
    for h in range(2):
        sources, targets, rank = slot_ranks(child_map[h], row_count)
        lands = (child_map[h] // row_count)[:, None] == jnp.arange(local_rows, dtype=jnp.int32)[None, :]
        lands = (lands & (targets == row_dev)[:, None]).astype(jnp.int32)
        slot = sources * (2 * CAP) + h * CAP + rank
        landed = jnp.sum(lands, axis=0)
        slots.append(jnp.where(landed > 0, jnp.sum(lands * slot[:, None], axis=0), -1))
        turned = jnp.sum(lands[:, :, None] * row_order[h][:, None, :], axis=0)
        orders.append(jnp.where((landed > 0)[:, None], turned, -1))
    slots = jnp.stack(slots)
    orders = jnp.stack(orders)

    def exchange(packed):
        arrived = lax.all_to_all(packed, "row", split_axis=0, concat_axis=0, tiled=True)
        return arrived.reshape((row_count * 2 * CAP,) + packed.shape[3:])

    kids = children.reshape(2, lrc, tile, local_cols, tile)
    near = kids[:, :, :, :lead_cols].reshape(2, lrc, tile, lead_cols * tile)
    near = exchange(pack_children(ids, child_map, near, row_count))
    far = pack_children(ids, child_map, kids, row_count)
    near, far = lax.optimization_barrier((near, far))
    fronts = [front_matrix[:, 0, :, b, 0, :] for b in range(lead_cols)]
    high, low = assemble_panel(fronts, orders.transpose(1, 0, 2), jnp.maximum(slots, 0), near)

    places = lead_slots(row_count, col_count, lead_rows, lead_cols)
    lead = jnp.stack([high[a, b].astype(F32) + low[a, b].astype(F32) for a, b in places]).astype(LINK)
    lead = lax.all_gather(lead, "col")
    height = local_rows - first
    parts = [merge_columns(gather_columns(high, 0, first, col_count, col_dev), 0, height, col_count)]
    lead = lax.all_gather(lead, "row")
    lead, far = lax.optimization_barrier((lead, far))
    far = exchange(far)
    blocks = list(unpack_lead(lead.reshape(-1, tile, tile).astype(F32), row_count, col_count, places))
    if lead_cols > 1:
        later, blocks[0] = lax.optimization_barrier((high, blocks[0]))
        late = gather_columns(later, lead_cols - 1, first, col_count, col_dev)

    diagonals, inverses, inverses_b, lower, lower_b = [], [], [], {}, {}
    sent = []
    for s in range(STEPS):
        if s == STEPS - 1:
            picked = column_rows(parts[0], first, local_cols, row_count, col_count, col_dev)
            blocks[0], picked, far = lax.optimization_barrier((blocks[0], picked, far))
            sent.append(from_owner_row(picked, row_count, col_count, row_dev, col_dev))
        c, v, vb = factor_block(blocks[0])
        diagonals.append(c)
        inverses.append(v)
        inverses_b.append(vb)
        left = STEPS - 1 - s
        if left:
            index = lambda t, u: t * (t + 1) // 2 + u
            below = [blocks[index(t, 0)] for t in range(1, left + 1)]
            trail = [blocks[index(t, u)] for t in range(1, left + 1) for u in range(1, t + 1)]
            low_f, low_b, blocks = advance(v, below, trail)
            blocks = list(blocks)
            for n in range(left):
                lower[s + 1 + n, s] = low_f[n]
                lower_b[s + 1 + n, s] = low_b[n]
    triangle = [
        diagonals[t] if t == u else lower[t, u] for t in range(STEPS) for u in range(t + 1)
    ]
    below_b = [lower_b[t, u] for t in range(1, STEPS) for u in range(t)]

    solved = [solve_rows(parts[0], None, 0, below_b, inverses_b)]
    if lead_cols > 1:
        late, inverses_b[-1], solved[0] = lax.optimization_barrier((late, inverses_b[-1], solved[0]))
        parts.append(merge_columns(late, lead_cols - 1, height, col_count))
        picked = column_rows(parts[-1], first, local_cols, row_count, col_count, col_dev)
        inverses_b[-1], picked = lax.optimization_barrier((inverses_b[-1], picked))
        sent.append(from_owner_row(picked, row_count, col_count, row_dev, col_dev))
        solved.append(
            solve_rows(parts[1], solved[0], parts[0].shape[0] // PWT, below_b, inverses_b)
        )
    schur_part = final_update(
        ids,
        slots,
        jnp.maximum(orders, 0),
        sent,
        below_b,
        inverses_b,
        far,
        solved,
        first,
        front,
        row_count,
        col_count,
    )

    low, parts = lax.optimization_barrier((low, parts))
    rest = low.reshape((col_count, share) + low.shape[1:])
    rest = lax.all_to_all(rest, "col", split_axis=0, concat_axis=0, tiled=True)
    mine = []
    for b, p in enumerate(parts):
        upper = jnp.stack(
            [
                lax.dynamic_index_in_dim(p, jnp.maximum(col_dev * share + k - first, 0), 1, False)
                for k in range(share)
            ],
            axis=1,
        )
        mine.append(upper.astype(F32) + rest[: p.shape[0], :, b].astype(F32))
    factor_part = own_rows(ids, jnp.concatenate(mine, axis=0), triangle, inverses, row_count)

    return (
        schur_part.reshape(front_matrix.shape),
        factor_part.reshape(share, 1, tile, TILES * tile),
    )


def solution(mesh):
    placed = (
        P(None, "row", None, None, "col", None),
        P(None, None, "row", None, None, "col", None),
        P(),
        P(),
    )
    return jax.shard_map(
        shards,
        mesh=mesh,
        in_specs=placed,
        out_specs=(P(None, "row", None, None, "col", None), P("col", "row", None, None)),
        check_vma=False,
    )
```

```python
import functools

import jax
import jax.numpy as jnp
from jax import lax
from jax.experimental import pallas as pl
from jax.experimental.pallas import tpu as pltpu
from jax.sharding import PartitionSpec as P

PWT = 4
STEPS = 3
CAP = 2
TILES = PWT * STEPS
F32 = jnp.float32
BF16 = jnp.bfloat16
LINK = jnp.float16
VMEM_LIMIT = 60 * 1024 * 1024


def slot_ranks(mapping, row_count):
    indices = jnp.arange(mapping.shape[0], dtype=jnp.int32)
    sources = indices % row_count
    targets = mapping % row_count
    earlier = (
        (sources[:, None] == sources[None, :])
        & (targets[:, None] == targets[None, :])
        & (indices[None, :] < indices[:, None])
    )
    return (sources, targets, jnp.sum(earlier.astype(jnp.int32), axis=1))


def dot(a, b, contract):
    return lax.dot_general(a, b, (contract, ((), ())), preferred_element_type=F32)


NT = ((1,), (1,))
NN = ((1,), (0,))
TN = ((0,), (0,))


def halves(x):
    high = x.astype(BF16)
    return high, (x - high.astype(F32)).astype(BF16)


def dot3(a, b, contract):
    ah, al = halves(a)
    bh, bl = halves(b)
    return dot(ah, bh, contract) + (dot(al, bh, contract) + dot(ah, bl, contract))


def spread_lane(x, j):
    return jnp.broadcast_to(x[:, j : j + 1], (8, x.shape[1]))


def spread_row(x, i):
    return jnp.broadcast_to(x[i : i + 1, :], (8, x.shape[1]))


def factor_tile(tile):
    size = tile.shape[0]
    sub = lax.broadcasted_iota(jnp.int32, (8, size), 0)
    lane = lax.broadcasted_iota(jnp.int32, (8, size), 1)
    groups = size // 8
    left = [tile[8 * s : 8 * s + 8] for s in range(groups)]
    right = [jnp.where(lane == sub + 8 * s, 1.0, 0.0).astype(F32) for s in range(groups)]
    for s in range(groups):
        columns = [spread_lane(left[s], 8 * s + b) for b in range(8)]
        square = {(a, b): spread_row(columns[b], a) for a in range(8) for b in range(a + 1)}
        lrow = [spread_row(left[s], i) for i in range(8)]
        rrow = [spread_row(right[s], i) for i in range(8)]
        more = s + 1 < groups
        ahead = [spread_lane(left[s + 1], 8 * s + b) for b in range(8)] if more else None
        new_left = jnp.zeros((8, size), F32)
        new_right = jnp.zeros((8, size), F32)
        for i in range(8):
            inverse = lax.rsqrt(square[i, i])
            below = {a: square[a, i] * inverse for a in range(i + 1, 8)}
            lrow[i] = lrow[i] * inverse
            rrow[i] = rrow[i] * inverse
            if more:
                ahead[i] = ahead[i] * inverse
            for a in range(i + 1, 8):
                for b in range(i + 1, a + 1):
                    square[a, b] = square[a, b] - below[a] * below[b]
                lrow[a] = lrow[a] - below[a] * lrow[i]
                rrow[a] = rrow[a] - below[a] * rrow[i]
                if more:
                    ahead[a] = ahead[a] - below[a] * ahead[i]
            new_left = jnp.where(sub == i, lrow[i], new_left)
            new_right = jnp.where(sub == i, rrow[i], new_right)
        left[s], right[s] = new_left, new_right
        if more:
            for a in range(8):
                left[s + 1] = left[s + 1] - ahead[a] * lrow[a]
                right[s + 1] = right[s + 1] - ahead[a] * rrow[a]
        if s + 2 < groups:
            both = dot3(new_left, jnp.concatenate([new_left, new_right], 1), TN)
            for t in range(s + 2, groups):
                left[t] = left[t] - both[8 * t : 8 * t + 8, :size]
                right[t] = right[t] - both[8 * t : 8 * t + 8, size:]
    return jnp.concatenate(left, 0), jnp.concatenate(right, 0)


def whole(shape):
    return pl.BlockSpec(shape, lambda *_: (0,) * len(shape), pipeline_mode=pl.Buffered(1))


def pack_kernel(row_count, ids_ref, map_ref, kids_ref, out_ref):
    out_ref[...] = jnp.zeros(out_ref.shape, out_ref.dtype)
    for h in range(2):
        targets = []
        for i in range(kids_ref.shape[1]):
            target = map_ref[h, i * row_count + ids_ref[0]] % row_count
            rank = jnp.int32(0)
            for earlier in targets:
                rank = rank + (earlier == target).astype(jnp.int32)
            targets.append(target)
            out_ref[target, h, rank] = kids_ref[h, i]


def pack_children(ids, child_map, kids, row_count):
    return pl.pallas_call(
        functools.partial(pack_kernel, row_count),
        out_shape=jax.ShapeDtypeStruct((row_count, 2, CAP) + kids.shape[2:], kids.dtype),
        grid_spec=pltpu.PrefetchScalarGridSpec(
            num_scalar_prefetch=2,
            grid=(1,),
            in_specs=[whole(kids.shape)],
            out_specs=whole((row_count, 2, CAP) + kids.shape[2:]),
        ),
        compiler_params=pltpu.CompilerParams(vmem_limit_bytes=VMEM_LIMIT),
    )(ids, child_map, kids)


def panel_kernel(lpc, share, slot_ref, *refs):
    fronts = refs[:lpc]
    order_ref, recv_ref, high_ref, low_ref = refs[lpc:]
    tile = high_ref.shape[-1]
    rows = lax.broadcasted_iota(jnp.int32, (tile, tile), 0)
    for k in range(share):
        a = pl.program_id(0) * share + k
        moved = jnp.zeros((tile, lpc * tile), F32)
        for h in range(2):
            pick = (rows == order_ref[k, h : h + 1, :]).astype(BF16)
            moved = moved + dot(pick, recv_ref[slot_ref[h, a]], NN)
        for b in range(lpc):
            high, low = halves(fronts[b][k] + moved[:, b * tile : (b + 1) * tile])
            high_ref[k, b] = high
            low_ref[k, b] = low


def assemble_panel(fronts, order, slots, received):
    local_rows, tile, _ = fronts[0].shape
    lpc = len(fronts)
    share = 4 if local_rows % 4 == 0 else 1
    out = (local_rows, lpc, tile, tile)
    return pl.pallas_call(
        functools.partial(panel_kernel, lpc, share),
        out_shape=(jax.ShapeDtypeStruct(out, BF16), jax.ShapeDtypeStruct(out, BF16)),
        grid_spec=pltpu.PrefetchScalarGridSpec(
            num_scalar_prefetch=1,
            grid=(local_rows // share,),
            in_specs=[pl.BlockSpec((share, tile, tile), lambda a, s: (a, 0, 0))] * lpc
            + [
                pl.BlockSpec((share, 2, tile), lambda a, s: (a, 0, 0)),
                whole(received.shape),
            ],
            out_specs=[pl.BlockSpec((share,) + out[1:], lambda a, s: (a, 0, 0, 0))] * 2,
        ),
        compiler_params=pltpu.CompilerParams(vmem_limit_bytes=VMEM_LIMIT),
    )(slots, *fronts, order, received)


def lead_slots(row_count, col_count, lead_rows, lead_cols):
    return [
        (a, b)
        for a in range(lead_rows)
        for b in range(lead_cols)
        if col_count * b <= row_count * a + row_count - 1 and col_count * b < TILES
    ]


def unpack_kernel(row_count, col_count, slots, g_ref, *blocks):
    tile = g_ref.shape[-1]
    place = {ab: n for n, ab in enumerate(slots)}
    for i in range(TILES):
        for j in range(i + 1):
            n = place[i // row_count, j // col_count]
            t, u = i // PWT, j // PWT
            rows = pl.ds((i % PWT) * tile, tile)
            cols = pl.ds((j % PWT) * tile, tile)
            source = ((i % row_count) * col_count + j % col_count) * len(slots) + n
            blocks[t * (t + 1) // 2 + u][rows, cols] = g_ref[source]


def unpack_lead(gathered, row_count, col_count, slots):
    width = PWT * gathered.shape[-1]
    count = STEPS * (STEPS + 1) // 2
    return pl.pallas_call(
        functools.partial(unpack_kernel, row_count, col_count, slots),
        out_shape=[jax.ShapeDtypeStruct((width, width), F32)] * count,
        compiler_params=pltpu.CompilerParams(vmem_limit_bytes=VMEM_LIMIT),
    )(gathered)


def block_kernel(d_ref, l_ref, v_ref, vb_ref, work):
    width = d_ref.shape[0]
    tile = width // PWT
    row = lax.broadcasted_iota(jnp.int32, (tile, tile), 0)
    col = lax.broadcasted_iota(jnp.int32, (tile, tile), 1)
    work[...] = d_ref[...]
    l_ref[...] = jnp.zeros((width, width), F32)
    v_ref[...] = jnp.zeros((width, width), F32)
    for k in range(PWT):
        low, high = k * tile, (k + 1) * tile
        block = work[low:high, low:high]
        block = jnp.where(row >= col, block, block.T)
        upper, inverse = factor_tile(block)
        l_ref[low:high, low:high] = jnp.where(row <= col, upper, 0.0).T
        if k > 0:
            v_ref[low:high, 0:low] = dot3(inverse, v_ref[low:high, 0:low], NN)
        v_ref[low:high, low:high] = inverse
        if k < PWT - 1:
            below = dot3(work[high:width, low:high], inverse, NT)
            l_ref[high:width, low:high] = below
            work[high:width, high:width] -= dot3(below, below, NT)
            v_ref[high:width, 0:high] -= dot3(below, v_ref[low:high, 0:high], NN)
    vb_ref[...] = v_ref[...].astype(BF16)


def factor_block(diagonal):
    shape = diagonal.shape
    return pl.pallas_call(
        block_kernel,
        out_shape=(
            jax.ShapeDtypeStruct(shape, F32),
            jax.ShapeDtypeStruct(shape, F32),
            jax.ShapeDtypeStruct(shape, BF16),
        ),
        scratch_shapes=[pltpu.VMEM(shape, F32)],
        compiler_params=pltpu.CompilerParams(vmem_limit_bytes=VMEM_LIMIT),
        cost_estimate=pl.CostEstimate(flops=3 * 10**10, bytes_accessed=4 * 10**6, transcendentals=0),
    )(diagonal)


def advance_kernel(count, v_ref, *refs):
    below, trail = refs[:count], refs[count : count + count * (count + 1) // 2]
    rest = refs[count + len(trail) :]
    lower, lower_b, out = rest[:count], rest[count : 2 * count], rest[2 * count :]
    for t in range(count):
        lower[t][...] = dot3(below[t][...], v_ref[...], NT)
        lower_b[t][...] = lower[t][...].astype(BF16)
    for t in range(count):
        for u in range(t + 1):
            n = t * (t + 1) // 2 + u
            out[n][...] = trail[n][...] - dot3(lower[t][...], lower[u][...], NT)


def advance(inverse, below, trail):
    count = len(below)
    shape = inverse.shape
    kinds = [F32] * count + [BF16] * count + [F32] * len(trail)
    out = pl.pallas_call(
        functools.partial(advance_kernel, count),
        out_shape=[jax.ShapeDtypeStruct(shape, k) for k in kinds],
        compiler_params=pltpu.CompilerParams(vmem_limit_bytes=VMEM_LIMIT),
        cost_estimate=pl.CostEstimate(flops=3 * 10**9, bytes_accessed=10**7, transcendentals=0),
    )(inverse, *below, *trail)
    return out[:count], out[count : 2 * count], out[2 * count :]


def side_by_side(parts):
    return jnp.concatenate([p.reshape(-1, p.shape[-1]) for p in parts], axis=1)


def own_kernel(row_count, ids_ref, own_ref, *refs):
    lower, inverse, out_ref = refs[: STEPS * (STEPS + 1) // 2], refs[-1 - STEPS : -1], refs[-1]
    share, tile = own_ref.shape[1:3]
    width = PWT * tile
    solved = []
    for s in range(STEPS):
        rest = side_by_side([own_ref[s * PWT + j] for j in range(PWT)])
        for q in range(s):
            rest = rest - dot3(solved[q], lower[s * (s + 1) // 2 + q][...], NT)
        solved.append(dot3(rest, inverse[s][...], NT))
        out_ref[:, s * width : (s + 1) * width] = solved[s]
    for k in range(share):
        index = (ids_ref[1] * share + k) * row_count + ids_ref[0]
        for t in range(STEPS):

            @pl.when(index // PWT == t)
            def _(k=k, t=t, index=index):
                source = pl.ds(pl.multiple_of((index % PWT) * tile, tile), tile)
                target = pl.ds(k * tile, tile)
                for s in range(STEPS):
                    if s <= t:
                        value = lower[t * (t + 1) // 2 + s][source, :]
                    else:
                        value = jnp.zeros((tile, width), F32)
                    out_ref[target, s * width : (s + 1) * width] = value


def own_rows(ids, own, lower, inverse, row_count):
    share, tile = own.shape[1:3]
    out = (share * tile, TILES * tile)
    return pl.pallas_call(
        functools.partial(own_kernel, row_count),
        out_shape=jax.ShapeDtypeStruct(out, F32),
        grid_spec=pltpu.PrefetchScalarGridSpec(
            num_scalar_prefetch=1,
            grid=(1,),
            in_specs=[whole(x.shape) for x in (own, *lower, *inverse)],
            out_specs=whole(out),
        ),
        compiler_params=pltpu.CompilerParams(vmem_limit_bytes=VMEM_LIMIT),
        cost_estimate=pl.CostEstimate(flops=6 * 10**9, bytes_accessed=15 * 10**6, transcendentals=0),
    )(ids, own, *lower, *inverse)


def solve_into(parts, lower, inverse, target, first):
    tile = parts[0].shape[-1]
    width = PWT * tile
    count = parts[0].shape[1]
    step = min(4, count)
    where = [(n, j) for n, ref in enumerate(parts) for j in range(ref.shape[0])]
    if first:
        target[0 : first * tile, :] = jnp.zeros((first * tile, target.shape[1]), BF16)

    @pl.loop(0, -(-count // step))
    def _(i):
        a = jnp.minimum(i * step, count - step)
        rows = pl.ds(pl.multiple_of((a + first) * tile, tile), step * tile)
        done = []
        for s in range(STEPS):
            rest = side_by_side([parts[n][j, pl.ds(a, step)] for n, j in where[s * PWT : (s + 1) * PWT]])
            if s > 0:
                rest = rest.astype(F32)
                for q in range(s):
                    rest = rest - dot(done[q], lower[s * (s - 1) // 2 + q][...], NT)
                rest = rest.astype(BF16)
            done.append(dot(rest, inverse[s][...], NT).astype(BF16))
            target[rows, s * width : (s + 1) * width] = done[s]


BELOW = STEPS * (STEPS - 1) // 2


def solve_kernel(begin, end, step, *refs):
    row_refs, refs = refs[:step], refs[step:]
    known, blocks, out_ref = refs[: min(begin, 1)], refs[min(begin, 1) : -1], refs[-1]
    lower, inverse = blocks[:BELOW], blocks[BELOW:]
    width = PWT * row_refs[0].shape[-1]
    done = [known[0][:, q * width : (q + 1) * width] for q in range(begin)]
    for s in range(begin, end):
        columns = range((s - begin) * PWT, (s - begin + 1) * PWT)
        rest = jnp.concatenate([side_by_side([ref[j] for j in columns]) for ref in row_refs], axis=0)
        if s > 0:
            rest = rest.astype(F32)
            for q in range(s):
                rest = rest - dot(done[q], lower[s * (s - 1) // 2 + q][...], NT)
            rest = rest.astype(BF16)
        done.append(dot(rest, inverse[s][...], NT).astype(BF16))
        out_ref[:, (s - begin) * width : (s - begin + 1) * width] = done[s]


def solve_rows(part, known, begin, lower, inverse):
    tile = part.shape[-1]
    step = 4
    steps = -(-part.shape[1] // step)
    end = begin + part.shape[0] // PWT
    width = PWT * tile
    rows = step * tile
    known = [known] if begin else []
    held = (*lower, *inverse)

    def row_tile(k):
        last = part.shape[1] - 1
        return pl.BlockSpec(
            (part.shape[0], 1, tile, tile), lambda i: (0, jnp.minimum(i * step + k, last), 0, 0)
        )

    return pl.pallas_call(
        functools.partial(solve_kernel, begin, end, step),
        out_shape=jax.ShapeDtypeStruct((steps * rows, (end - begin) * width), BF16),
        grid=(steps,),
        in_specs=[row_tile(k) for k in range(step)]
        + [pl.BlockSpec((rows, k.shape[1]), lambda i: (i, 0)) for k in known]
        + [whole(x.shape) for x in held],
        out_specs=pl.BlockSpec((rows, (end - begin) * width), lambda i: (i, 0)),
        compiler_params=pltpu.CompilerParams(vmem_limit_bytes=VMEM_LIMIT),
        cost_estimate=pl.CostEstimate(
            flops=2 * steps * rows * (end - begin) * width * end * width,
            bytes_accessed=4 * part.size,
            transcendentals=0,
        ),
    )(*[part] * step, *known, *held)


def final_kernel(row_count, col_count, n_parts, ids_ref, slot_ref, order_ref, *refs):
    parts, blocks = refs[:n_parts], refs[n_parts : n_parts + BELOW + STEPS]
    rest = refs[n_parts + BELOW + STEPS :]
    front_ref, out_ref, xc_ref, xr_ref = rest[-4:]
    g = pl.program_id(0)
    tile = out_ref.shape[-1]
    share = xr_ref.shape[0] // tile
    kid_refs, row_refs = rest[: 2 * share], rest[2 * share : -4]
    for n, ref in enumerate(row_refs):
        k = n % share
        left = 0 if n < share else row_refs[0].shape[1]
        xr_ref[k * tile : (k + 1) * tile, left : left + ref.shape[1]] = ref[...]
    local_cols = xc_ref.shape[0] // tile

    @pl.when(g == 0)
    def _():
        solve_into(parts, blocks[:BELOW], blocks[BELOW:], xc_ref, local_cols - parts[0].shape[1])

    out_ref[...] = front_ref[...]
    for k in range(share):
        a = g * share + k
        for h in range(2):
            slot = slot_ref[h, a]

            @pl.when(slot >= 0)
            def _(a=a, k=k, h=h):
                @pl.loop(0, tile, unroll=8)
                def _(t):
                    at = (k * tile + order_ref[h, a, t]) * local_cols
                    at = pl.ds(pl.multiple_of(at, local_cols), local_cols)
                    out_ref[at, :] += kid_refs[2 * k + h][0, t].astype(F32)

    last = row_count * (g * share + share - 1) + ids_ref[0]
    pair = 2 if local_cols % 2 == 0 else 1
    for b in range(0, local_cols, pair):
        some = last >= jnp.maximum(col_count * b + ids_ref[1], TILES)

        @pl.when(some)
        def _(b=b):
            update = dot(xr_ref[...], xc_ref[b * tile : (b + pair) * tile, :], NT)
            for k in range(share):
                row_tile = row_count * (g * share + k) + ids_ref[0]
                for j in range(pair):
                    col_tile = col_count * (b + j) + ids_ref[1]
                    keep = (row_tile >= col_tile) & (col_tile >= TILES)
                    at = pl.ds(k * tile * local_cols + b + j, tile, stride=local_cols)
                    part = update[k * tile : (k + 1) * tile, j * tile : (j + 1) * tile]
                    out_ref[at, :] = jnp.where(keep, out_ref[at, :] - part, 0.0)

        @pl.when(jnp.logical_not(some))
        def _(b=b):
            for j in range(pair):
                out_ref[pl.ds(b + j, share * tile, stride=local_cols), :] = jnp.zeros(
                    (share * tile, tile), F32
                )


def final_update(
    ids, slots, order, parts, lower, inverse, received, solved, first, front, row_count, col_count
):
    rows = front.shape[0] // col_count
    tile = front.shape[1]
    share = slots.shape[1] // col_count
    wide = sum(x.shape[1] for x in solved)
    block = pl.BlockSpec((rows, tile), lambda g, *_: (g, 0))
    held = (*parts, *lower, *inverse)

    def kid_tile(k, h):
        return pl.BlockSpec(
            (1,) + received.shape[1:],
            lambda g, ids, slots, order: (jnp.maximum(slots[h, g * share + k], 0), 0, 0, 0),
        )

    def row_tile(k, x):
        return pl.BlockSpec(
            (tile, x.shape[1]), lambda g, *_: (jnp.maximum(g * share + k - first, 0), 0)
        )

    return pl.pallas_call(
        functools.partial(final_kernel, row_count, col_count, len(parts)),
        out_shape=jax.ShapeDtypeStruct(front.shape, F32),
        grid_spec=pltpu.PrefetchScalarGridSpec(
            num_scalar_prefetch=3,
            grid=(col_count,),
            in_specs=[whole(x.shape) for x in held]
            + [kid_tile(k, h) for k in range(share) for h in range(2)]
            + [row_tile(k, x) for x in solved for k in range(share)]
            + [block],
            out_specs=block,
            scratch_shapes=[
                pltpu.VMEM((received.shape[2] * tile, wide), BF16),
                pltpu.VMEM((share * tile, wide), BF16),
            ],
        ),
        compiler_params=pltpu.CompilerParams(vmem_limit_bytes=VMEM_LIMIT),
        cost_estimate=pl.CostEstimate(
            flops=2 * slots.shape[1] * tile * wide * wide, bytes_accessed=8 * front.size, transcendentals=0
        ),
    )(
        ids,
        slots,
        order,
        *held,
        *[received] * (2 * share),
        *[x for x in solved for _ in range(share)],
        front,
    )


def column_rows(part, first, local_cols, row_count, col_count, col_dev):
    fold = col_count // row_count
    begin = TILES // col_count
    part = jnp.pad(part, ((0, 0), (first - fold * begin, 0), (0, 0), (0, 0)))
    split = part.reshape(part.shape[0], local_cols - begin, fold, part.shape[2], part.shape[3])
    picked = split[:, :, 0]
    for f in range(1, fold):
        picked = jnp.where(col_dev // row_count == f, split[:, :, f], picked)
    return picked


def from_owner_row(own, row_count, col_count, row_dev, col_dev, gate=None):
    away = row_dev ^ (col_dev % row_count)
    stride = row_count // 2
    while stride:
        pairs = []
        for r in range(row_count):
            for c in range(col_count):
                if (r ^ (c % row_count)) % (2 * stride) == 0:
                    pairs.append((r * col_count + c, (r ^ stride) * col_count + c))
        arrived = lax.ppermute(own, ("row", "col"), pairs)
        if gate is not None:
            arrived, gate = lax.optimization_barrier((arrived, gate))
        own = jnp.where(away % (2 * stride) == stride, arrived, own)
        stride //= 2
    return own


def gather_columns(panel, b, first, col_count, col_dev):
    rows = panel[first:, b]
    n = rows.shape[0]
    count = min(col_count, TILES - col_count * b)
    if b > 0 and 2 * count == col_count:
        half = (n + 1) // 2
        sent = lax.ppermute(rows[n - half :], "col", [(c, c + count) for c in range(count)])
        rows = jnp.where(col_dev < count, rows[:half], sent)
    return lax.all_gather(rows, "col")


def merge_columns(gathered, b, n, col_count):
    count = min(col_count, TILES - col_count * b)
    half = gathered.shape[1]
    if half < n:
        return jnp.concatenate([gathered[:count], gathered[count:, 2 * half - n :]], axis=1)
    return gathered[:count]


def shards(front_matrix, children, child_map, row_order):
    row_count = lax.axis_size("row")
    col_count = lax.axis_size("col")
    row_dev = lax.axis_index("row")
    col_dev = lax.axis_index("col")
    local_rows = front_matrix.shape[0]
    tile = front_matrix.shape[2]
    local_cols = front_matrix.shape[3]
    lrc = children.shape[1]
    lead_cols = -(-TILES // col_count)
    lead_rows = -(-TILES // row_count)
    first = TILES // row_count
    share = local_rows // col_count
    front = front_matrix.reshape(local_rows * tile * local_cols, tile)
    ids = jnp.stack([row_dev, col_dev]).astype(jnp.int32)

    slots, orders = [], []
    for h in range(2):
        sources, targets, rank = slot_ranks(child_map[h], row_count)
        lands = (child_map[h] // row_count)[:, None] == jnp.arange(local_rows, dtype=jnp.int32)[None, :]
        lands = (lands & (targets == row_dev)[:, None]).astype(jnp.int32)
        slot = sources * (2 * CAP) + h * CAP + rank
        landed = jnp.sum(lands, axis=0)
        slots.append(jnp.where(landed > 0, jnp.sum(lands * slot[:, None], axis=0), -1))
        turned = jnp.sum(lands[:, :, None] * row_order[h][:, None, :], axis=0)
        orders.append(jnp.where((landed > 0)[:, None], turned, -1))
    slots = jnp.stack(slots)
    orders = jnp.stack(orders)

    def exchange(packed):
        arrived = lax.all_to_all(packed, "row", split_axis=0, concat_axis=0, tiled=True)
        return arrived.reshape((row_count * 2 * CAP,) + packed.shape[3:])

    kids = children.reshape(2, lrc, tile, local_cols, tile)
    near = kids[:, :, :, :lead_cols].reshape(2, lrc, tile, lead_cols * tile)
    near = exchange(pack_children(ids, child_map, near, row_count))
    far = pack_children(ids, child_map, kids, row_count)
    near, far = lax.optimization_barrier((near, far))
    fronts = [front_matrix[:, 0, :, b, 0, :] for b in range(lead_cols)]
    high, low = assemble_panel(fronts, orders.transpose(1, 0, 2), jnp.maximum(slots, 0), near)

    places = lead_slots(row_count, col_count, lead_rows, lead_cols)
    lead = jnp.stack([high[a, b].astype(F32) + low[a, b].astype(F32) for a, b in places]).astype(LINK)
    lead = lax.all_gather(lead, "col")
    height = local_rows - first
    parts = [merge_columns(gather_columns(high, 0, first, col_count, col_dev), 0, height, col_count)]
    lead = lax.all_gather(lead, "row")
    lead, far = lax.optimization_barrier((lead, far))
    far = exchange(far)
    blocks = list(unpack_lead(lead.reshape(-1, tile, tile).astype(F32), row_count, col_count, places))
    if lead_cols > 1:
        later, blocks[0] = lax.optimization_barrier((high, blocks[0]))
        late = gather_columns(later, lead_cols - 1, first, col_count, col_dev)

    diagonals, inverses, inverses_b, lower, lower_b = [], [], [], {}, {}
    sent = []
    for s in range(STEPS):
        if s == STEPS - 1:
            picked = column_rows(parts[0], first, local_cols, row_count, col_count, col_dev)
            blocks[0], picked, far = lax.optimization_barrier((blocks[0], picked, far))
            sent.append(from_owner_row(picked, row_count, col_count, row_dev, col_dev))
        c, v, vb = factor_block(blocks[0])
        diagonals.append(c)
        inverses.append(v)
        inverses_b.append(vb)
        left = STEPS - 1 - s
        if left:
            index = lambda t, u: t * (t + 1) // 2 + u
            below = [blocks[index(t, 0)] for t in range(1, left + 1)]
            trail = [blocks[index(t, u)] for t in range(1, left + 1) for u in range(1, t + 1)]
            low_f, low_b, blocks = advance(v, below, trail)
            blocks = list(blocks)
            for n in range(left):
                lower[s + 1 + n, s] = low_f[n]
                lower_b[s + 1 + n, s] = low_b[n]
    triangle = [
        diagonals[t] if t == u else lower[t, u] for t in range(STEPS) for u in range(t + 1)
    ]
    below_b = [lower_b[t, u] for t in range(1, STEPS) for u in range(t)]

    solved = [solve_rows(parts[0], None, 0, below_b, inverses_b)]
    if lead_cols > 1:
        late, inverses_b[-1], solved[0] = lax.optimization_barrier((late, inverses_b[-1], solved[0]))
        parts.append(merge_columns(late, lead_cols - 1, height, col_count))
        picked = column_rows(parts[-1], first, local_cols, row_count, col_count, col_dev)
        inverses_b[-1], picked = lax.optimization_barrier((inverses_b[-1], picked))
        solved.append(
            solve_rows(parts[1], solved[0], parts[0].shape[0] // PWT, below_b, inverses_b)
        )
        sent.append(from_owner_row(picked, row_count, col_count, row_dev, col_dev, solved[1]))
    schur_part = final_update(
        ids,
        slots,
        jnp.maximum(orders, 0),
        sent,
        below_b,
        inverses_b,
        far,
        solved,
        first,
        front,
        row_count,
        col_count,
    )

    low, parts = lax.optimization_barrier((low, parts))
    rest = low.reshape((col_count, share) + low.shape[1:])
    rest = lax.all_to_all(rest, "col", split_axis=0, concat_axis=0, tiled=True)
    mine = []
    for b, p in enumerate(parts):
        upper = jnp.stack(
            [
                lax.dynamic_index_in_dim(p, jnp.maximum(col_dev * share + k - first, 0), 1, False)
                for k in range(share)
            ],
            axis=1,
        )
        mine.append(upper.astype(F32) + rest[: p.shape[0], :, b].astype(F32))
    factor_part = own_rows(ids, jnp.concatenate(mine, axis=0), triangle, inverses, row_count)

    return (
        schur_part.reshape(front_matrix.shape),
        factor_part.reshape(share, 1, tile, TILES * tile),
    )


def solution(mesh):
    placed = (
        P(None, "row", None, None, "col", None),
        P(None, None, "row", None, None, "col", None),
        P(),
        P(),
    )
    return jax.shard_map(
        shards,
        mesh=mesh,
        in_specs=placed,
        out_specs=(P(None, "row", None, None, "col", None), P("col", "row", None, None)),
        check_vma=False,
    )
```
